256 devices in a mesh: gx: 32 (over y_lo, z, core), gy: 8 (over x, y_hi).
Axes of the slice: x: 4, y: 4 (y_hi: 2, y_lo: 2; y = y_hi * 2 + y_lo), z: 8, core: 2. Of those that a mesh axis runs over, the one named last changes fastest.
Arguments:
- velocity: float32 [3, 256, 256, 128], P(None, 'gx', 'gy'), may hold values from -6 to 6
- lm_old: float32 [256, 256, 128], P('gx', 'gy'), may hold values from 0.1 to 10
- mm_old: float32 [256, 256, 128], P('gx', 'gy'), may hold values from 2 to 50
- upstream: int32 [2, 256, 256, 128], P(None, 'gx', 'gy'), may hold values from -3 to 3
- point_pos: float32 [32, 8, 3, 576], P('gx', 'gy'), may hold values from 0 to 128, as said below
- point_coef: float32 [32, 8, 576], P('gx', 'gy'), may hold values from 0.005 to 0.05
- tile_turbines: int32 [32, 8], P('gx', 'gy'), may hold values from 1 to 3, as said below
Outputs:
- lm_next: float32 [256, 256, 128], P('gx', 'gy')
- mm_next: float32 [256, 256, 128], P('gx', 'gy')
- eddy_visc: float32 [256, 256, 128], P('gx', 'gy')
- body_force: float32 [3, 256, 256, 128], P(None, 'gx', 'gy')
The draws below stay inside these ranges and needn't reach their ends.
Inputs may be any that keep to these rules, and one draw needn't show every extreme that they name: `point_pos`: turbine t of a tile owns slots t * 3 * 64 to (t + 1) * 3 * 64 - 1; its points lie on three blades of radius 12 in a plane of constant x. Every point lies inside its own tile: 0 <= x < 8, 0 < y < 32, and z is within 14 of 64. `tile_turbines`: slots beyond 3 * 64 times a tile's count are unused. Every tile holds at least one turbine; some tile holds 3.
All inputs are finite; a program needn't handle non-finite values.
Results may differ from the reference program's by a relative error of at most 0.0003.
Values sent between devices are 32-bit elements; how exact they have to be, the bound alone decides.
No kernel may reach another device: no remote copies, remote signals or barrier semaphores. Data moves between devices by JAX's collectives and lax.ppermute only.
A program may use at most 128 MiB of HBM per device.

```python
import math
import jax
import jax.numpy as jnp
from jax import lax

CX = 8
CY = 32
NZ = 128
TMAX = 3
BLADE_PTS = 64
ROTOR = 12
PCAP = 576
TILES_X = 32
TILES_Y = 8
NX = 256
NY = 256


def draw_point_pos(key, part):
    keys = jax.random.split(jax.random.fold_in(key, 11), 4)
    shape = (TILES_X, TILES_Y, TMAX)
    hub_x = jax.random.uniform(keys[0], shape, jnp.float32, 0.5, CX - 0.5)
    hub_y = jax.random.uniform(keys[1], shape, jnp.float32, ROTOR + 1.0, CY - ROTOR - 1.0)
    hub_z = NZ / 2.0 + jax.random.uniform(keys[2], shape, jnp.float32, -2.0, 2.0)
    phase = jax.random.uniform(keys[3], shape, jnp.float32, 0.0, 2.0 * math.pi)
    radius = (jnp.arange(BLADE_PTS, dtype=jnp.float32) + 0.5) / BLADE_PTS * ROTOR
    angle = phase[..., None] + 2.0 * math.pi * jnp.arange(3, dtype=jnp.float32) / 3.0
    along_y = hub_y[..., None, None] + radius * jnp.sin(angle[..., None])
    along_z = hub_z[..., None, None] + radius * jnp.cos(angle[..., None])
    along_x = jnp.broadcast_to(hub_x[..., None, None], along_y.shape)
    stacked = jnp.stack([along_x, along_y, along_z], axis=2)
    return stacked.reshape(TILES_X, TILES_Y, 3, PCAP).astype(jnp.float32)


def draw_tile_turbines(key, part):
    keys = jax.random.split(jax.random.fold_in(key, 23), 2)
    counts = jax.random.randint(keys[0], (TILES_X, TILES_Y), 1, TMAX + 1)
    chosen = jax.random.randint(keys[1], (), 0, TILES_X * TILES_Y)
    marker = jnp.arange(TILES_X * TILES_Y, dtype=jnp.int32).reshape(TILES_X, TILES_Y) == chosen
    return jnp.where(marker, TMAX, counts).astype(jnp.int32)


def set_ends(values, stream_key, smallest, largest):
    index_at = [jax.random.randint(jax.random.fold_in(stream_key, axis), (), 0, length) for axis, length in enumerate(values.shape)]
    longest = values.shape.index(max(values.shape))
    neighbour = index_at[:longest] + [(index_at[longest] + 1) % values.shape[longest]] + index_at[longest + 1:]
    return values.at[tuple(index_at)].set(smallest).at[tuple(neighbour)].set(largest)


def shard_levels(stream_key, extent, cuts, least, largest):
    gain = 1.0
    for axis_at, parts in cuts:
        heights = jax.random.uniform(jax.random.fold_in(jax.random.fold_in(stream_key, 6), axis_at), (parts,), jnp.float32, least / len(cuts), largest / len(cuts))
        gain = gain * jnp.repeat(jnp.exp(heights), extent[axis_at] // parts).reshape((-1,) + (1,) * (len(extent) - 1 - axis_at))
    return gain


def gaussian(stream_key, dims, width, limit, cuts=(), kind=jnp.bfloat16):
    result = width * jax.random.normal(stream_key, dims, jnp.float32)
    if cuts:
        result = result * shard_levels(stream_key, dims, cuts, -0.22, 0.18)
    return jnp.clip(result, -limit, limit).astype(kind)


def setup_inputs(seed: int = 0) -> dict:
    splits = jax.random.split(jax.random.key(seed), 8)
    velocity = gaussian(splits[0], (3, NX, NY, NZ), 1.0, 6.0, ((1, 32), (2, 8)), jnp.float32)
    lm_old = jnp.clip(jnp.exp(math.log(10.0) - 4.6051702 * jax.random.uniform(splits[1], (NX, NY, NZ), jnp.float32) ** shard_levels(splits[1], (NX, NY, NZ), ((0, 32), (1, 8)), -0.2, 0.2)), 0.1, 10.0)
    mm_old = jnp.clip(jnp.exp(math.log(50.0) - 3.218876 * jax.random.uniform(splits[2], (NX, NY, NZ), jnp.float32) ** shard_levels(splits[2], (NX, NY, NZ), ((0, 32), (1, 8)), -0.2, 0.2)), 2.0, 50.0)
    upstream = set_ends(jax.random.randint(splits[3], (2, NX, NY, NZ), -3, 4), jax.random.fold_in(splits[3], 1), -3, 3).astype(jnp.int32)
    point_pos = draw_point_pos(jax.random.fold_in(splits[7], 71), 0)
    point_coef = jnp.clip(jnp.exp(math.log(0.05) - 2.3025851 * jax.random.uniform(splits[5], (TILES_X, TILES_Y, PCAP), jnp.float32) ** shard_levels(splits[5], (TILES_X, TILES_Y, PCAP), ((0, 32), (1, 8)), -0.2, 0.2)), 0.005, 0.05)
    tile_turbines = draw_tile_turbines(jax.random.fold_in(splits[7], 71), 0)
    return {"velocity": velocity, "lm_old": lm_old, "mm_old": mm_old, "upstream": upstream, "point_pos": point_pos, "point_coef": point_coef, "tile_turbines": tile_turbines}


time_step = 0.2
kernel_width = 1.5
pair_list = ((0, 0), (1, 1), (2, 2), (0, 1), (0, 2), (1, 2))

def pair_weights():
    return jnp.array([1.0, 1.0, 1.0, 2.0, 2.0, 2.0], dtype=jnp.float32).reshape(6, 1, 1, 1)

def deriv_x(values):
    return 0.5 * (values[..., 2:, 1:-1, :] - values[..., :-2, 1:-1, :])

def deriv_y(values):
    return 0.5 * (values[..., 1:-1, 2:, :] - values[..., 1:-1, :-2, :])

def deriv_z(values):
    padded = jnp.concatenate([values[..., :1], values, values[..., -1:]], axis=-1)
    return 0.5 * (padded[..., 1:-1, 1:-1, 2:] - padded[..., 1:-1, 1:-1, :-2])

def test_filter(values):
    partial_x = 0.25 * values[..., :-2, :, :] + 0.5 * values[..., 1:-1, :, :] + 0.25 * values[..., 2:, :, :]
    return 0.25 * partial_x[..., :-2, :] + 0.5 * partial_x[..., 1:-1, :] + 0.25 * partial_x[..., 2:, :]

def trim_rim(values):
    return values[..., 1:-1, 1:-1, :]

def strain_rate(flow):
    slopes = (deriv_x(flow), deriv_y(flow), deriv_z(flow))
    tensor = jnp.stack([0.5 * (slopes[col_comp][row_comp] + slopes[row_comp][col_comp]) for row_comp, col_comp in pair_list])
    magnitude = jnp.sqrt(2.0 * lax.optimization_barrier(jnp.sum(pair_weights() * tensor * tensor, axis=0)))
    return (tensor, magnitude)

def closure_terms(velocity_ext):
    wide = trim_rim(velocity_ext)
    strain_wide, magnitude_wide = strain_rate(wide)
    product_hat = test_filter(magnitude_wide * strain_wide)
    velocity_hat = test_filter(wide)
    strain_hat, magnitude_hat = strain_rate(velocity_hat)
    inner = trim_rim(wide)
    moments = jnp.stack([inner[row_comp] * inner[col_comp] for row_comp, col_comp in pair_list])
    hat_inner = trim_rim(velocity_hat)
    leonard = test_filter(moments) - jnp.stack([hat_inner[row_comp] * hat_inner[col_comp] for row_comp, col_comp in pair_list])
    model_tensor = 2.0 * (product_hat - 4.0 * magnitude_hat * strain_hat)
    weights = pair_weights()
    lm_term = lax.optimization_barrier(jnp.sum(weights * leonard * model_tensor, axis=0))
    mm_term = lax.optimization_barrier(jnp.sum(weights * model_tensor * model_tensor, axis=0))
    return (lm_term, mm_term, trim_rim(magnitude_wide))

def lagrange_update(lm_term, mm_term, smagnitude, lm_up, mm_up):
    memory = 1.5 * (lm_up * mm_up) ** (-0.125)
    ratio = time_step / memory
    relax = ratio / (1.0 + ratio)
    lm_next = jnp.maximum(relax * lm_term + (1.0 - relax) * lm_up, 0.0)
    mm_next = relax * mm_term + (1.0 - relax) * mm_up
    return (lm_next, mm_next, lm_next / mm_next * smagnitude)

def kernel(offset):
    return jnp.maximum(jnp.exp(-(offset / kernel_width) ** 2) - math.exp(-4.0), 0.0)

def window(position, tile, span, total):
    start = jnp.floor(position) - 2.0
    cells = start[:, None] + jnp.arange(6, dtype=jnp.int32).astype(jnp.float32)
    weights = kernel(cells - position[:, None])
    where_at = (tile[:, None] * span + cells.astype(jnp.int32)) % total
    return (weights, where_at)

def reference(velocity, lm_old, mm_old, upstream, point_pos, point_coef, tile_turbines):

    def slab_terms(row):
        rows = (row * CX - 3 + jnp.arange(CX + 6, dtype=jnp.int32)) % NX
        slab = jnp.take(velocity, rows, axis=1)
        slab = jnp.concatenate([slab[:, :, NY - 3:], slab, slab[:, :, :3]], axis=2)
        return closure_terms(slab)
    lm_term, mm_term, smagnitude = lax.map(slab_terms, jnp.arange(TILES_X, dtype=jnp.int32))
    lm_term = lm_term.reshape(NX, NY, NZ)
    mm_term = mm_term.reshape(NX, NY, NZ)
    smagnitude = smagnitude.reshape(NX, NY, NZ)
    rows = (jnp.arange(NX, dtype=jnp.int32)[:, None, None] - upstream[0]) % NX
    cols = (jnp.arange(NY, dtype=jnp.int32)[None, :, None] - upstream[1]) % NY
    levels = jnp.arange(NZ, dtype=jnp.int32)[None, None, :]
    flat = (rows * NY + cols) * NZ + levels
    lm_up = jnp.take(lm_old.reshape(-1), flat)
    mm_up = jnp.take(mm_old.reshape(-1), flat)
    lm_next, mm_next, eddy_visc = lagrange_update(lm_term, mm_term, smagnitude, lm_up, mm_up)
    live = jnp.arange(PCAP, dtype=jnp.int32)[None, None, :] < tile_turbines[:, :, None] * (3 * BLADE_PTS)
    strength = jnp.where(live, point_coef, 0.0).reshape(-1)
    tile_x = jnp.broadcast_to(jnp.arange(TILES_X, dtype=jnp.int32)[:, None, None], (TILES_X, TILES_Y, PCAP)).reshape(-1)
    tile_y = jnp.broadcast_to(jnp.arange(TILES_Y, dtype=jnp.int32)[None, :, None], (TILES_X, TILES_Y, PCAP)).reshape(-1)
    weight_x, where_x = window(point_pos[:, :, 0].reshape(-1), tile_x, CX, NX)
    weight_y, where_y = window(point_pos[:, :, 1].reshape(-1), tile_y, CY, NY)
    weight_z, where_z = window(point_pos[:, :, 2].reshape(-1), jnp.zeros_like(tile_x), 0, NZ)
    local = velocity[:, where_x[:, :, None, None], where_y[:, None, :, None], where_z[:, None, None, :]]
    sampled = jnp.einsum('cqabe,qa,qb,qe->cq', local, weight_x, weight_y, weight_z, precision=lax.Precision.HIGHEST)
    speed = jnp.sqrt(lax.optimization_barrier(jnp.sum(sampled * sampled, axis=0)))
    point_force = -(strength * speed) * sampled
    kernel_cube = weight_x[:, :, None, None] * weight_y[:, None, :, None] * weight_z[:, None, None, :]
    spread = point_force[:, :, None, None, None] * kernel_cube[None]
    body_force = jnp.zeros((3, NX, NY, NZ), jnp.float32).at[:, where_x[:, :, None, None], where_y[:, None, :, None], where_z[:, None, None, :]].add(spread)
    return (lm_next, mm_next, eddy_visc, body_force)
```

```python
import math

import jax
import jax.numpy as jnp
from jax import lax
from jax.experimental import pallas as pl
from jax.experimental.pallas import tpu as pltpu
from jax.sharding import PartitionSpec as P

F32 = jnp.float32
CX, CY, NZ = 8, 32, 128
TURBINES, SLOTS = 3, 192
ZLOW, ZSPAN = 46, 40
XMSG = 504
YMSG = 320
YA, YU, YP = 72, 156, 248
EY = 40
PY = 48


def shifted(block, axis, distance):
    count = lax.axis_size(axis)
    return lax.ppermute(block, axis, [(i, (i + distance) % count) for i in range(count)])


def weight(offset):
    scaled = offset * (1.0 / 1.5)
    return jnp.maximum(jnp.exp(-(scaled * scaled)) - math.exp(-4.0), 0.0)


def packed(parts):
    lane = lax.broadcasted_iota(jnp.int32, parts[0].shape, 1)
    first = pltpu.roll(parts[0], NZ - ZLOW, 1)
    second = pltpu.roll(parts[1], NZ + ZSPAN - ZLOW, 1)
    third = pltpu.roll(parts[2], 2 * ZSPAN - ZLOW, 1)
    rest = jnp.where(lane < 3 * ZSPAN, third, 0.0)
    return jnp.where(lane < ZSPAN, first, jnp.where(lane < 2 * ZSPAN, second, rest))


def pack_x(vel, lm, mm, pos, coef, count, low, high, slab, points):
    for row in range(CX):
        parts = [vel[pl.ds((c * CX + row) * CY, CY), :] for c in range(3)]
        slab[pl.ds(row * CY, CY), :] = packed(parts)
    for out, first_v, first_a, first_u in ((low, 0, 0, 2), (high, CX - 2, CX - 3, CX - 5)):
        for c in range(3):
            out[pl.ds(c * 64, 64), :] = vel[pl.ds((c * CX + first_v) * CY, 64), :]
        out[pl.ds(192, 96), :] = lm[pl.ds(first_a * CY, 96), :]
        out[pl.ds(288, 96), :] = mm[pl.ds(first_a * CY, 96), :]
        out[pl.ds(384, 96), :] = slab[pl.ds(first_u * CY, 96), :]
    lane = lax.broadcasted_iota(jnp.int32, (1, 128), 1)
    turbines = count[0, 0]
    for t in range(TURBINES):
        rows = []
        for values in (pos[1:2, :], pos[2:3, :], coef[0:1, :]):
            rows.append(values[:, t * SLOTS : t * SLOTS + 128])
            rows.append(values[:, t * SLOTS + 64 : t * SLOTS + 192])
        live = jnp.where(t < turbines, 1.0, 0.0)
        rows[4] = rows[4] * live
        rows[5] = jnp.where(lane < 64, 0.0, rows[5] * live)
        rows.append(pos[0:1, t * SLOTS : t * SLOTS + 128])
        rows.append(jnp.zeros((1, 128), F32))
        block = jnp.concatenate(rows, axis=0)
        for out, base in ((low, 480), (high, 480), (points, 0)):
            out[pl.ds(base + 8 * t, 8), :] = block


def pack_y(vel, lm, mm, slab, points, xlow, xhigh, low, high, ulow, uhigh):
    for out, message in ((ulow, xlow), (uhigh, xhigh)):
        for i in range(2):
            parts = [message[pl.ds(c * 64 + i * CY, CY), :] for c in range(3)]
            out[pl.ds(i * CY, CY), :] = packed(parts)
    for out, col_v, col_a, col_u in ((low, 0, 0, 0), (high, CY - 2, CY - 3, CY - 5)):
        for c in range(3):
            for j in range(2):
                base, col = (c * 2 + j) * 12, col_v + j
                out[pl.ds(base, 8), :] = vel[pl.ds(c * 256 + col, 8, stride=CY), :]
                out[pl.ds(base + 8, 2), :] = xlow[pl.ds(c * 64 + col, 2, stride=CY), :]
                out[pl.ds(base + 10, 2), :] = xhigh[pl.ds(c * 64 + col, 2, stride=CY), :]
        for f, own in enumerate((lm, mm)):
            for j in range(3):
                base, col = YA + (f * 3 + j) * 14, col_a + j
                out[pl.ds(base, 8), :] = own[pl.ds(col, 8, stride=CY), :]
                out[pl.ds(base + 8, 3), :] = xlow[pl.ds(192 + f * 96 + col, 3, stride=CY), :]
                out[pl.ds(base + 11, 3), :] = xhigh[pl.ds(192 + f * 96 + col, 3, stride=CY), :]
        for j in range(5):
            base, col = YU + j * 18, col_u + j
            out[pl.ds(base, 8), :] = slab[pl.ds(col, 8, stride=CY), :]
            out[pl.ds(base + 8, 3), :] = xlow[pl.ds(384 + col, 3, stride=CY), :]
            out[pl.ds(base + 11, 2), :] = ulow[pl.ds(col, 2, stride=CY), :]
            out[pl.ds(base + 13, 2), :] = uhigh[pl.ds(col, 2, stride=CY), :]
            out[pl.ds(base + 15, 3), :] = xhigh[pl.ds(384 + col, 3, stride=CY), :]
        out[pl.ds(YU + 90, 2), :] = jnp.zeros((2, 128), F32)
        for k, source in enumerate((points, xlow, xhigh)):
            first = 0 if k == 0 else 480
            out[pl.ds(YP + 24 * k, 24), :] = source[pl.ds(first, 24), :]


def assemble(vel, lm, mm, slab, xlow, xhigh, ylow, yhigh, ulow, uhigh, ev, ea, eu):
    def rows_v(c, row):
        return (c * 12 + row + 2) * EY

    def rows_a(f, row):
        return (f * 14 + row + 3) * EY

    for c in range(3):
        for row in range(CX):
            ev[pl.ds(rows_v(c, row) + 4, CY), :] = vel[pl.ds((c * CX + row) * CY, CY), :]
        for i in range(2):
            ev[pl.ds(rows_v(c, i - 2) + 4, CY), :] = xlow[pl.ds(c * 64 + i * CY, CY), :]
            ev[pl.ds(rows_v(c, i + 8) + 4, CY), :] = xhigh[pl.ds(c * 64 + i * CY, CY), :]
        for message, first in ((ylow, 2), (yhigh, 36)):
            for j in range(2):
                base, col = (c * 2 + j) * 12, first + j
                ev[pl.ds(rows_v(c, 0) + col, 8, stride=EY), :] = message[pl.ds(base, 8), :]
                ev[pl.ds(rows_v(c, -2) + col, 2, stride=EY), :] = message[pl.ds(base + 8, 2), :]
                ev[pl.ds(rows_v(c, 8) + col, 2, stride=EY), :] = message[pl.ds(base + 10, 2), :]
    for f, own in enumerate((lm, mm)):
        for row in range(CX):
            ea[pl.ds(rows_a(f, row) + 4, CY), :] = own[pl.ds(row * CY, CY), :]
        for i in range(3):
            source = 192 + f * 96 + i * CY
            ea[pl.ds(rows_a(f, i - 3) + 4, CY), :] = xlow[pl.ds(source, CY), :]
            ea[pl.ds(rows_a(f, i + 8) + 4, CY), :] = xhigh[pl.ds(source, CY), :]
        for message, first in ((ylow, 1), (yhigh, 36)):
            for j in range(3):
                base, col = YA + (f * 3 + j) * 14, first + j
                ea[pl.ds(rows_a(f, 0) + col, 8, stride=EY), :] = message[pl.ds(base, 8), :]
                ea[pl.ds(rows_a(f, -3) + col, 3, stride=EY), :] = message[pl.ds(base + 8, 3), :]
                ea[pl.ds(rows_a(f, 8) + col, 3, stride=EY), :] = message[pl.ds(base + 11, 3), :]
    zero = jnp.zeros((8, 128), F32)
    for row in range(18):
        eu[pl.ds(row * PY, 8), :] = zero
        eu[pl.ds(row * PY + 40, 8), :] = zero
    for row in range(CX):
        eu[pl.ds((row + 5) * PY + 8, CY), :] = slab[pl.ds(row * CY, CY), :]
    for i in range(3):
        eu[pl.ds(i * PY + 8, CY), :] = xlow[pl.ds(384 + i * CY, CY), :]
        eu[pl.ds((i + 15) * PY + 8, CY), :] = xhigh[pl.ds(384 + i * CY, CY), :]
    for i in range(2):
        eu[pl.ds((i + 3) * PY + 8, CY), :] = ulow[pl.ds(i * CY, CY), :]
        eu[pl.ds((i + 13) * PY + 8, CY), :] = uhigh[pl.ds(i * CY, CY), :]
    for message, first in ((ylow, 3), (yhigh, 40)):
        for j in range(5):
            base, col = YU + j * 18, first + j
            eu[pl.ds(5 * PY + col, 8, stride=PY), :] = message[pl.ds(base, 8), :]
            eu[pl.ds(col, 3, stride=PY), :] = message[pl.ds(base + 8, 3), :]
            eu[pl.ds(3 * PY + col, 2, stride=PY), :] = message[pl.ds(base + 11, 2), :]
            eu[pl.ds(13 * PY + col, 2, stride=PY), :] = message[pl.ds(base + 13, 2), :]
            eu[pl.ds(15 * PY + col, 3, stride=PY), :] = message[pl.ds(base + 15, 3), :]


PAIRS = ((0, 0), (1, 1), (2, 2), (0, 1), (0, 2), (1, 2))


def slope_z(values):
    lane = lax.broadcasted_iota(jnp.int32, values.shape, 1)
    above = jnp.where(lane == NZ - 1, values, pltpu.roll(values, NZ - 1, 1))
    below = jnp.where(lane == 0, values, pltpu.roll(values, 1, 1))
    return above - below


def tensor_of(slopes):
    parts = [slopes[0][0], slopes[1][1], slopes[2][2]]
    parts += [slopes[j][i] + slopes[i][j] for i, j in PAIRS[3:]]
    diag = parts[0] * parts[0] + parts[1] * parts[1] + parts[2] * parts[2]
    off = parts[3] * parts[3] + parts[4] * parts[4] + parts[5] * parts[5]
    return parts, jnp.sqrt(2.0 * diag + off)


def closure_first(ev, xs, mags):
    def at(c, row, col):
        return ev[pl.ds((c * 12 + row + 2) * EY + col + 4, 8), :]

    def put(q, row, col, value):
        xs[pl.ds((q * 10 + row + 1) * EY + col + 4, 8), :] = value

    for col in (-2, 6, 14, 22, 26):
        before = [at(c, -2, col) for c in range(3)]
        here = [at(c, -1, col) for c in range(3)]
        history = []
        for row in range(-1, 9):
            after = [at(c, row + 1, col) for c in range(3)]
            slopes = [
                [after[c] - before[c] for c in range(3)],
                [at(c, row, col + 1) - at(c, row, col - 1) for c in range(3)],
                [slope_z(here[c]) for c in range(3)],
            ]
            parts, mag = tensor_of(slopes)
            now = [mag * part for part in parts] + [here[i] * here[j] for i, j in PAIRS]
            if 0 <= row < CX:
                mags[pl.ds(row * EY + col + 4, 8), :] = mag
            for c in range(3):
                put(12 + c, row, col, before[c] + (here[c] + here[c]) + after[c])
            history.append(now)
            if len(history) == 3:
                for q in range(12):
                    value = history[0][q] + (history[1][q] + history[1][q]) + history[2][q]
                    put(q, row - 1, col, value)
                history.pop(0)
            before, here = here, after


def closure_hat(xs, uh):
    for c in range(3):
        for row in range(-1, 9):
            base = ((12 + c) * 10 + row + 1) * EY + 4
            for col in (-1, 7, 15, 23, 25):
                mid = xs[pl.ds(base + col, 8), :]
                value = xs[pl.ds(base + col - 1, 8), :] + (mid + mid) + xs[pl.ds(base + col + 1, 8), :]
                uh[pl.ds((c * 10 + row + 1) * EY + col + 4, 8), :] = value


def take_rows(values, index):
    return jnp.take_along_axis(values, index, axis=0)


def averages_up(ea, up, row, col):
    sub = lax.broadcasted_iota(jnp.int32, (8, 128), 0)
    shift_x = up[pl.ds(row * CY + col, 8), :]
    index = sub - up[pl.ds((CX + row) * CY + col, 8), :] + 3
    early = index < 8
    first = jnp.minimum(index, 7)
    second = jnp.maximum(index - 6, 0)
    result = [None, None]
    for shift in range(-3, 4):
        chosen = shift_x == shift
        for f in range(2):
            base = (f * 14 + row - shift + 3) * EY + 4 + col
            value = jnp.where(
                early,
                take_rows(ea[pl.ds(base - 3, 8), :], first),
                take_rows(ea[pl.ds(base + 3, 8), :], second),
            )
            result[f] = value if result[f] is None else jnp.where(chosen, value, result[f])
    return result


def closure_last(ea, up, xs, uh, mags, lm_next, mm_next, visc):
    def summed(q, row, col):
        base = (q * 10 + row + 1) * EY + 4 + col
        mid = xs[pl.ds(base, 8), :]
        return xs[pl.ds(base - 1, 8), :] + (mid + mid) + xs[pl.ds(base + 1, 8), :]

    def hat(c, row, col):
        return uh[pl.ds((c * 10 + row + 1) * EY + 4 + col, 8), :]

    for row in range(CX):
        for col in range(0, CY, 8):
            here = [hat(c, row, col) for c in range(3)]
            slopes = [
                [hat(c, row + 1, col) - hat(c, row - 1, col) for c in range(3)],
                [hat(c, row, col + 1) - hat(c, row, col - 1) for c in range(3)],
                [slope_z(here[c]) for c in range(3)],
            ]
            parts, mag = tensor_of(slopes)
            mag = 0.25 * mag
            lm_sum = diag = off = None
            for q, (i, j) in enumerate(PAIRS):
                model = summed(q, row, col) - mag * parts[q]
                leonard = summed(6 + q, row, col) - (1.0 / 16.0) * (here[i] * here[j])
                term = leonard * model
                lm_sum = term if lm_sum is None else lm_sum + term
                square = model * model
                if q < 3:
                    diag = square if diag is None else diag + square
                else:
                    off = square if off is None else off + square
            lm_term = lm_sum * (1.0 / 512.0)
            mm_term = (2.0 * diag + off) * (1.0 / 2048.0)
            lm_up, mm_up = averages_up(ea, up, row, col)
            ratio = (0.2 / 1.5) * jnp.sqrt(jnp.sqrt(jnp.sqrt(lm_up * mm_up)))
            inverse = 1.0 / (1.0 + ratio)
            lm_new = jnp.maximum((ratio * lm_term + lm_up) * inverse, 0.0)
            mm_new = (ratio * mm_term + mm_up) * inverse
            out = pl.ds(row * CY + col, 8)
            lm_next[out, :] = lm_new
            mm_next[out, :] = mm_new
            visc[out, :] = lm_new / mm_new * (0.5 * mags[pl.ds(row * EY + col + 4, 8), :])


def dot_over(a, b, dims):
    return lax.dot_general(
        a, b, (dims, ((), ())), precision=lax.Precision.HIGHEST, preferred_element_type=F32
    )


def turbine(block, dx, dy, eu, total):
    if dy == 0:
        first, span, out_first, out_span = 0, PY, 8, CY
    elif dy < 0:
        first, span, out_first, out_span = 0, 16, 8, 8
    else:
        first, span, out_first, out_span = 32, 16, 32, 8
    in_rows = {0: range(-2, 11), -1: range(-5, 3), 1: range(6, 13)}[dx]
    out_rows = {0: range(0, 8), -1: range(0, 3), 1: range(6, 8)}[dx]
    cell_x = lax.broadcasted_iota(jnp.int32, (24, 128), 0).astype(F32) - 5.0
    weight_x = weight(cell_x - (block[6:7, :] + float(dx * CX)))
    plane = None
    for row in in_rows:
        term = weight_x[row + 5 : row + 6, :] * eu[pl.ds((row + 5) * PY + first, span), :]
        plane = term if plane is None else plane + term
    pos_y = jnp.concatenate([block[0:1, :], block[1:2, :]], axis=1) + float(dy * CY)
    pos_z = jnp.concatenate([block[2:3, :], block[3:4, :]], axis=1)
    strength = jnp.concatenate([block[4:5, :], block[5:6, :]], axis=1)
    cell_y = lax.broadcasted_iota(jnp.int32, (span, 256), 0).astype(F32) + float(first - 8)
    cell_z = lax.broadcasted_iota(jnp.int32, (ZSPAN, 256), 0).astype(F32) + float(ZLOW)
    weight_y = weight(cell_y - pos_y)
    weight_z = weight(cell_z - pos_z)
    columns = dot_over(plane, weight_y, ((0,), (0,)))
    sampled = [
        jnp.sum(columns[c * ZSPAN : (c + 1) * ZSPAN, :] * weight_z, axis=0, keepdims=True)
        for c in range(3)
    ]
    speed = jnp.sqrt(sampled[0] * sampled[0] + sampled[1] * sampled[1] + sampled[2] * sampled[2])
    scale = -(strength * speed)
    spread = [weight_z * (scale * sampled[c]) for c in range(3)]
    spread = jnp.concatenate(spread + [jnp.zeros((8, 256), F32)], axis=0)
    rows_y = weight_y[out_first - first : out_first - first + out_span, :]
    patch = dot_over(rows_y, spread, ((1,), (1,)))
    for row in out_rows:
        where_at = pl.ds(row * CY + out_first - 8, out_span)
        total[where_at, :] += weight_x[row + 5 : row + 6, :] * patch


def main_kernel(
    vel, lm, mm, up, slab, points, xlow, xhigh, ylow, yhigh, ulow, uhigh,
    lm_next, mm_next, visc, body, ev, ea, eu, xs, uh, mags, total,
):
    assemble(vel, lm, mm, slab, xlow, xhigh, ylow, yhigh, ulow, uhigh, ev, ea, eu)
    closure_first(ev, xs, mags)
    closure_hat(xs, uh)
    closure_last(ea, up, xs, uh, mags, lm_next, mm_next, visc)
    total[...] = jnp.zeros((CX * CY, 128), F32)
    for dx, source, base in ((0, points, 0), (-1, xlow, 480), (1, xhigh, 480)):

        def column(t, carry, dx=dx, source=source, base=base):
            turbine(source[pl.ds(pl.multiple_of(base + t * 8, 8), 8), :], dx, 0, eu, total)
            return carry

        lax.fori_loop(0, TURBINES, column, 0)
    for dy, message in ((-1, ylow), (1, yhigh)):
        for k, dx in enumerate((0, -1, 1)):

            def rim(t, carry, dx=dx, dy=dy, message=message, k=k):
                block = message[pl.ds(pl.multiple_of(YP + k * 24 + t * 8, 8), 8), :]
                if dy < 0:
                    near = jnp.maximum(
                        jnp.where(block[4:5, :] > 0.0, block[0:1, :], 0.0),
                        jnp.where(block[5:6, :] > 0.0, block[1:2, :], 0.0),
                    )
                    reach = jnp.max(near) > float(CY - 3)
                else:
                    near = jnp.minimum(
                        jnp.where(block[4:5, :] > 0.0, block[0:1, :], float(CY)),
                        jnp.where(block[5:6, :] > 0.0, block[1:2, :], float(CY)),
                    )
                    reach = jnp.min(near) < 2.0

                @pl.when(reach)
                def _():
                    turbine(block, dx, dy, eu, total)

                return carry

            lax.fori_loop(0, TURBINES, rim, 0)
    lane = lax.broadcasted_iota(jnp.int32, (CY, 128), 1)
    inside = (lane >= ZLOW) & (lane < ZLOW + ZSPAN)
    for row in range(CX):
        values = total[pl.ds(row * CY, CY), :]
        for c, shift in enumerate((ZLOW, NZ + ZLOW - ZSPAN, NZ + ZLOW - 2 * ZSPAN)):
            out = jnp.where(inside, pltpu.roll(values, shift % NZ, 1), 0.0)
            body[pl.ds((c * CX + row) * CY, CY), :] = out


VMEM = pl.BlockSpec(memory_space=pltpu.VMEM)


def rows(count):
    return jax.ShapeDtypeStruct((count, 128), F32)


def shards(velocity, lm_old, mm_old, upstream, point_pos, point_coef, tile_turbines):
    vel = velocity.reshape(3 * CX * CY, NZ)
    lm = lm_old.reshape(CX * CY, NZ)
    mm = mm_old.reshape(CX * CY, NZ)
    up = upstream.reshape(2 * CX * CY, NZ)
    low, high, slab, points = pl.pallas_call(
        pack_x,
        out_shape=(rows(XMSG), rows(XMSG), rows(CX * CY), rows(24)),
        in_specs=[VMEM] * 5 + [pl.BlockSpec(memory_space=pltpu.SMEM)],
        out_specs=(VMEM,) * 4,
        name="pack_x",
    )(vel, lm, mm, point_pos[0, 0], point_coef[0], tile_turbines)
    xlow = shifted(high, "gx", 1)
    xhigh = shifted(low, "gx", -1)
    low, high, ulow, uhigh = pl.pallas_call(
        pack_y,
        out_shape=(rows(YMSG), rows(YMSG), rows(64), rows(64)),
        in_specs=[VMEM] * 7,
        out_specs=(VMEM,) * 4,
        name="pack_y",
    )(vel, lm, mm, slab, points, xlow, xhigh)
    ylow = shifted(high, "gy", 1)
    yhigh = shifted(low, "gy", -1)
    lm_next, mm_next, visc, body = pl.pallas_call(
        main_kernel,
        out_shape=(rows(CX * CY), rows(CX * CY), rows(CX * CY), rows(3 * CX * CY)),
        in_specs=[VMEM] * 12,
        out_specs=(VMEM,) * 4,
        scratch_shapes=[
            pltpu.VMEM((3 * 12 * EY, 128), F32),
            pltpu.VMEM((2 * 14 * EY, 128), F32),
            pltpu.VMEM((18 * PY, 128), F32),
            pltpu.VMEM((15 * 10 * EY, 128), F32),
            pltpu.VMEM((3 * 10 * EY, 128), F32),
            pltpu.VMEM((CX * EY, 128), F32),
            pltpu.VMEM((CX * CY, 128), F32),
        ],
        name="main",
    )(vel, lm, mm, up, slab, points, xlow, xhigh, ylow, yhigh, ulow, uhigh)
    field = (CX, CY, NZ)
    return (
        lm_next.reshape(field),
        mm_next.reshape(field),
        visc.reshape(field),
        body.reshape(3, *field),
    )


def solution(mesh):
    return jax.shard_map(
        shards,
        mesh=mesh,
        in_specs=(
            P(None, "gx", "gy", None),
            P("gx", "gy", None),
            P("gx", "gy", None),
            P(None, "gx", "gy", None),
            P("gx", "gy", None, None),
            P("gx", "gy", None),
            P("gx", "gy"),
        ),
        out_specs=(
            P("gx", "gy", None),
            P("gx", "gy", None),
            P("gx", "gy", None),
            P(None, "gx", "gy", None),
        ),
        check_vma=False,
    )
```

```python
import math

import jax
import jax.numpy as jnp
from jax import lax
from jax.experimental import pallas as pl
from jax.experimental.pallas import tpu as pltpu
from jax.sharding import PartitionSpec as P

F32 = jnp.float32
CX, CY, NZ = 8, 32, 128
TURBINES, SLOTS = 3, 192
ZLOW, ZSPAN = 46, 40
XMSG = 504
YMSG = 320
YA, YU, YP = 72, 156, 248
EY = 40
PY = 48


def shifted(block, axis, distance):
    count = lax.axis_size(axis)
    return lax.ppermute(block, axis, [(i, (i + distance) % count) for i in range(count)])


def weight(offset):
    scaled = offset * (1.0 / 1.5)
    return jnp.maximum(jnp.exp(-(scaled * scaled)) - math.exp(-4.0), 0.0)


def packed(parts):
    lane = lax.broadcasted_iota(jnp.int32, parts[0].shape, 1)
    first = pltpu.roll(parts[0], NZ - ZLOW, 1)
    second = pltpu.roll(parts[1], NZ + ZSPAN - ZLOW, 1)
    third = pltpu.roll(parts[2], 2 * ZSPAN - ZLOW, 1)
    rest = jnp.where(lane < 3 * ZSPAN, third, 0.0)
    return jnp.where(lane < ZSPAN, first, jnp.where(lane < 2 * ZSPAN, second, rest))


def pack_x(vel, lm, mm, pos, coef, count, low, high, slab, points):
    for row in range(CX):
        parts = [vel[pl.ds((c * CX + row) * CY, CY), :] for c in range(3)]
        slab[pl.ds(row * CY, CY), :] = packed(parts)
    for out, first_v, first_a, first_u in ((low, 0, 0, 2), (high, CX - 2, CX - 3, CX - 5)):
        for c in range(3):
            out[pl.ds(c * 64, 64), :] = vel[pl.ds((c * CX + first_v) * CY, 64), :]
        out[pl.ds(192, 96), :] = lm[pl.ds(first_a * CY, 96), :]
        out[pl.ds(288, 96), :] = mm[pl.ds(first_a * CY, 96), :]
        out[pl.ds(384, 96), :] = slab[pl.ds(first_u * CY, 96), :]
    lane = lax.broadcasted_iota(jnp.int32, (1, 128), 1)
    turbines = count[0, 0]
    for t in range(TURBINES):
        rows = []
        for values in (pos[1], pos[2], coef[0:1, :]):
            rows.append(values[:, t * SLOTS : t * SLOTS + 128])
            rows.append(values[:, t * SLOTS + 64 : t * SLOTS + 192])
        live = jnp.where(t < turbines, 1.0, 0.0)
        rows[4] = rows[4] * live
        rows[5] = jnp.where(lane < 64, 0.0, rows[5] * live)
        rows.append(pos[0][:, t * SLOTS : t * SLOTS + 128])
        rows.append(jnp.zeros((1, 128), F32))
        block = jnp.concatenate(rows, axis=0)
        for out, base in ((low, 480), (high, 480), (points, 0)):
            out[pl.ds(base + 8 * t, 8), :] = block


def pack_y(vel, lm, mm, slab, points, xlow, xhigh, low, high, ulow, uhigh):
    for out, message in ((ulow, xlow), (uhigh, xhigh)):
        for i in range(2):
            parts = [message[pl.ds(c * 64 + i * CY, CY), :] for c in range(3)]
            out[pl.ds(i * CY, CY), :] = packed(parts)
    for out, col_v, col_a, col_u in ((low, 0, 0, 0), (high, CY - 2, CY - 3, CY - 5)):
        for c in range(3):
            for j in range(2):
                base, col = (c * 2 + j) * 12, col_v + j
                out[pl.ds(base, 8), :] = vel[pl.ds(c * 256 + col, 8, stride=CY), :]
                out[pl.ds(base + 8, 2), :] = xlow[pl.ds(c * 64 + col, 2, stride=CY), :]
                out[pl.ds(base + 10, 2), :] = xhigh[pl.ds(c * 64 + col, 2, stride=CY), :]
        for f, own in enumerate((lm, mm)):
            for j in range(3):
                base, col = YA + (f * 3 + j) * 14, col_a + j
                out[pl.ds(base, 8), :] = own[pl.ds(col, 8, stride=CY), :]
                out[pl.ds(base + 8, 3), :] = xlow[pl.ds(192 + f * 96 + col, 3, stride=CY), :]
                out[pl.ds(base + 11, 3), :] = xhigh[pl.ds(192 + f * 96 + col, 3, stride=CY), :]
        for j in range(5):
            base, col = YU + j * 18, col_u + j
            out[pl.ds(base, 8), :] = slab[pl.ds(col, 8, stride=CY), :]
            out[pl.ds(base + 8, 3), :] = xlow[pl.ds(384 + col, 3, stride=CY), :]
            out[pl.ds(base + 11, 2), :] = ulow[pl.ds(col, 2, stride=CY), :]
            out[pl.ds(base + 13, 2), :] = uhigh[pl.ds(col, 2, stride=CY), :]
            out[pl.ds(base + 15, 3), :] = xhigh[pl.ds(384 + col, 3, stride=CY), :]
        out[pl.ds(YU + 90, 2), :] = jnp.zeros((2, 128), F32)
        for k, source in enumerate((points, xlow, xhigh)):
            first = 0 if k == 0 else 480
            out[pl.ds(YP + 24 * k, 24), :] = source[pl.ds(first, 24), :]


def rows_v(c, row):
    return (c * 12 + row + 2) * EY


def rows_a(f, row):
    return (f * 14 + row + 3) * EY


def assemble(vel, lm, mm, slab, xlow, xhigh, ulow, uhigh, ev, ea, eu):
    for c in range(3):
        for row in range(CX):
            ev[pl.ds(rows_v(c, row) + 4, CY), :] = vel[pl.ds((c * CX + row) * CY, CY), :]
        for i in range(2):
            ev[pl.ds(rows_v(c, i - 2) + 4, CY), :] = xlow[pl.ds(c * 64 + i * CY, CY), :]
            ev[pl.ds(rows_v(c, i + 8) + 4, CY), :] = xhigh[pl.ds(c * 64 + i * CY, CY), :]
    for f, own in enumerate((lm, mm)):
        for row in range(CX):
            ea[pl.ds(rows_a(f, row) + 4, CY), :] = own[pl.ds(row * CY, CY), :]
        for i in range(3):
            source = 192 + f * 96 + i * CY
            ea[pl.ds(rows_a(f, i - 3) + 4, CY), :] = xlow[pl.ds(source, CY), :]
            ea[pl.ds(rows_a(f, i + 8) + 4, CY), :] = xhigh[pl.ds(source, CY), :]
    zero = jnp.zeros((8, 128), F32)
    for row in range(18):
        eu[pl.ds(row * PY, 8), :] = zero
        eu[pl.ds(row * PY + 40, 8), :] = zero
    for row in range(CX):
        eu[pl.ds((row + 5) * PY + 8, CY), :] = slab[pl.ds(row * CY, CY), :]
    for i in range(3):
        eu[pl.ds(i * PY + 8, CY), :] = xlow[pl.ds(384 + i * CY, CY), :]
        eu[pl.ds((i + 15) * PY + 8, CY), :] = xhigh[pl.ds(384 + i * CY, CY), :]
    for i in range(2):
        eu[pl.ds((i + 3) * PY + 8, CY), :] = ulow[pl.ds(i * CY, CY), :]
        eu[pl.ds((i + 13) * PY + 8, CY), :] = uhigh[pl.ds(i * CY, CY), :]


def complete(ylow, yhigh, ev, ea, eu):
    for c in range(3):
        for message, first in ((ylow, 2), (yhigh, 36)):
            for j in range(2):
                base, col = (c * 2 + j) * 12, first + j
                ev[pl.ds(rows_v(c, 0) + col, 8, stride=EY), :] = message[pl.ds(base, 8), :]
                ev[pl.ds(rows_v(c, -2) + col, 2, stride=EY), :] = message[pl.ds(base + 8, 2), :]
                ev[pl.ds(rows_v(c, 8) + col, 2, stride=EY), :] = message[pl.ds(base + 10, 2), :]
    for f in range(2):
        for message, first in ((ylow, 1), (yhigh, 36)):
            for j in range(3):
                base, col = YA + (f * 3 + j) * 14, first + j
                ea[pl.ds(rows_a(f, 0) + col, 8, stride=EY), :] = message[pl.ds(base, 8), :]
                ea[pl.ds(rows_a(f, -3) + col, 3, stride=EY), :] = message[pl.ds(base + 8, 3), :]
                ea[pl.ds(rows_a(f, 8) + col, 3, stride=EY), :] = message[pl.ds(base + 11, 3), :]
    for message, first in ((ylow, 3), (yhigh, 40)):
        for j in range(5):
            base, col = YU + j * 18, first + j
            eu[pl.ds(5 * PY + col, 8, stride=PY), :] = message[pl.ds(base, 8), :]
            eu[pl.ds(col, 3, stride=PY), :] = message[pl.ds(base + 8, 3), :]
            eu[pl.ds(3 * PY + col, 2, stride=PY), :] = message[pl.ds(base + 11, 2), :]
            eu[pl.ds(13 * PY + col, 2, stride=PY), :] = message[pl.ds(base + 13, 2), :]
            eu[pl.ds(15 * PY + col, 3, stride=PY), :] = message[pl.ds(base + 15, 3), :]


PAIRS = ((0, 0), (1, 1), (2, 2), (0, 1), (0, 2), (1, 2))


def slope_z(values):
    lane = lax.broadcasted_iota(jnp.int32, values.shape, 1)
    above = jnp.where(lane == NZ - 1, values, pltpu.roll(values, NZ - 1, 1))
    below = jnp.where(lane == 0, values, pltpu.roll(values, 1, 1))
    return above - below


def tensor_of(slopes):
    parts = [slopes[0][0], slopes[1][1], slopes[2][2]]
    parts += [slopes[j][i] + slopes[i][j] for i, j in PAIRS[3:]]
    diag = parts[0] * parts[0] + parts[1] * parts[1] + parts[2] * parts[2]
    off = parts[3] * parts[3] + parts[4] * parts[4] + parts[5] * parts[5]
    return parts, jnp.sqrt(2.0 * diag + off)


def closure_first(ev, xs, mags, starts):
    def at(c, row, col):
        return ev[pl.ds((c * 12 + row + 2) * EY + col + 4, 8), :]

    def put(q, row, col, value):
        xs[pl.ds((q * 10 + row + 1) * EY + col + 4, 8), :] = value

    for col in starts:
        before = [at(c, -2, col) for c in range(3)]
        here = [at(c, -1, col) for c in range(3)]
        history = []
        for row in range(-1, 9):
            after = [at(c, row + 1, col) for c in range(3)]
            slopes = [
                [after[c] - before[c] for c in range(3)],
                [at(c, row, col + 1) - at(c, row, col - 1) for c in range(3)],
                [slope_z(here[c]) for c in range(3)],
            ]
            parts, mag = tensor_of(slopes)
            now = [mag * part for part in parts] + [here[i] * here[j] for i, j in PAIRS]
            if 0 <= row < CX:
                mags[pl.ds(row * EY + col + 4, 8), :] = mag
            for c in range(3):
                put(12 + c, row, col, before[c] + (here[c] + here[c]) + after[c])
            history.append(now)
            if len(history) == 3:
                for q in range(12):
                    value = history[0][q] + (history[1][q] + history[1][q]) + history[2][q]
                    put(q, row - 1, col, value)
                history.pop(0)
            before, here = here, after


def closure_hat(xs, uh, starts):
    for c in range(3):
        for row in range(-1, 9):
            base = ((12 + c) * 10 + row + 1) * EY + 4
            for col in starts:
                mid = xs[pl.ds(base + col, 8), :]
                value = xs[pl.ds(base + col - 1, 8), :] + (mid + mid) + xs[pl.ds(base + col + 1, 8), :]
                uh[pl.ds((c * 10 + row + 1) * EY + col + 4, 8), :] = value


def take_rows(values, index):
    return jnp.take_along_axis(values, index, axis=0)


def averages_up(ea, up, row, col):
    sub = lax.broadcasted_iota(jnp.int32, (8, 128), 0)
    shift_x = up[pl.ds(row * CY + col, 8), :]
    index = sub - up[pl.ds((CX + row) * CY + col, 8), :] + 3
    early = index < 8
    first = jnp.minimum(index, 7)
    second = jnp.maximum(index - 6, 0)
    result = [None, None]
    for shift in range(-3, 4):
        chosen = shift_x == shift
        for f in range(2):
            base = (f * 14 + row - shift + 3) * EY + 4 + col
            value = jnp.where(
                early,
                take_rows(ea[pl.ds(base - 3, 8), :], first),
                take_rows(ea[pl.ds(base + 3, 8), :], second),
            )
            result[f] = value if result[f] is None else jnp.where(chosen, value, result[f])
    return result


def closure_last(ea, up, xs, uh, mags, lm_next, mm_next, visc, starts):
    def summed(q, row, col):
        base = (q * 10 + row + 1) * EY + 4 + col
        mid = xs[pl.ds(base, 8), :]
        return xs[pl.ds(base - 1, 8), :] + (mid + mid) + xs[pl.ds(base + 1, 8), :]

    def hat(c, row, col):
        return uh[pl.ds((c * 10 + row + 1) * EY + 4 + col, 8), :]

    for row in range(CX):
        for col in starts:
            here = [hat(c, row, col) for c in range(3)]
            slopes = [
                [hat(c, row + 1, col) - hat(c, row - 1, col) for c in range(3)],
                [hat(c, row, col + 1) - hat(c, row, col - 1) for c in range(3)],
                [slope_z(here[c]) for c in range(3)],
            ]
            parts, mag = tensor_of(slopes)
            mag = 0.25 * mag
            lm_sum = diag = off = None
            for q, (i, j) in enumerate(PAIRS):
                model = summed(q, row, col) - mag * parts[q]
                leonard = summed(6 + q, row, col) - (1.0 / 16.0) * (here[i] * here[j])
                term = leonard * model
                lm_sum = term if lm_sum is None else lm_sum + term
                square = model * model
                if q < 3:
                    diag = square if diag is None else diag + square
                else:
                    off = square if off is None else off + square
            lm_term = lm_sum * (1.0 / 512.0)
            mm_term = (2.0 * diag + off) * (1.0 / 2048.0)
            lm_up, mm_up = averages_up(ea, up, row, col)
            ratio = (0.2 / 1.5) * jnp.sqrt(jnp.sqrt(jnp.sqrt(lm_up * mm_up)))
            inverse = 1.0 / (1.0 + ratio)
            lm_new = jnp.maximum((ratio * lm_term + lm_up) * inverse, 0.0)
            mm_new = (ratio * mm_term + mm_up) * inverse
            out = pl.ds(row * CY + col, 8)
            lm_next[out, :] = lm_new
            mm_next[out, :] = mm_new
            visc[out, :] = lm_new / mm_new * (0.5 * mags[pl.ds(row * EY + col + 4, 8), :])


def split(values):
    high = values.astype(jnp.bfloat16)
    return high, (values - high.astype(F32)).astype(jnp.bfloat16)


def dot_over(a, b, dims):
    (a_high, a_low), (b_high, b_low) = split(a), split(b)

    def dot(x, y):
        return lax.dot_general(x, y, (dims, ((), ())), preferred_element_type=F32)

    return dot(a_high, b_high) + dot(a_high, b_low) + dot(a_low, b_high)


def turbines(blocks, dx, dy, eu, total, skip_rim=False):
    if dy == 0:
        first, span, out_first, out_span = 0, PY, 8, CY
    elif dy < 0:
        first, span, out_first, out_span = 0, 16, 8, 8
    else:
        first, span, out_first, out_span = 32, 16, 32, 8
    in_rows = {0: range(-2, 11), -1: range(-5, 3), 1: range(6, 13)}[dx]
    out_rows = {0: range(0, 8), -1: range(0, 3), 1: range(6, 8)}[dx]
    cell_x = lax.broadcasted_iota(jnp.int32, (24, 128), 0).astype(F32) - 5.0
    cell_y = lax.broadcasted_iota(jnp.int32, (span, 256), 0).astype(F32) + float(first - 8)
    cell_z = lax.broadcasted_iota(jnp.int32, (ZSPAN, 256), 0).astype(F32) + float(ZLOW)
    weights_x = [weight(cell_x - (block[6:7, :] + float(dx * CX))) for block in blocks]
    planes = [None] * len(blocks)
    for row in in_rows:
        values = eu[pl.ds((row + 5) * PY + first, span), :]
        for t, weight_x in enumerate(weights_x):
            term = weight_x[row + 5 : row + 6, :] * values
            planes[t] = term if planes[t] is None else planes[t] + term
    patches = []
    for block, plane in zip(blocks, planes):
        pos_y = jnp.concatenate([block[0:1, :], block[1:2, :]], axis=1)
        pos_z = jnp.concatenate([block[2:3, :], block[3:4, :]], axis=1)
        strength = jnp.concatenate([block[4:5, :], block[5:6, :]], axis=1)
        if skip_rim:
            rim = (strength > 0.0) & ((pos_y < 2.0) | (pos_y > float(CY - 3)))
            strength = strength * (1.0 - jnp.max(rim.astype(F32), axis=1, keepdims=True))
        weight_y = weight(cell_y - (pos_y + float(dy * CY)))
        weight_z = weight(cell_z - pos_z)
        columns = dot_over(plane.T, weight_y, ((1,), (0,)))
        sampled = [
            jnp.sum(columns[c * ZSPAN : (c + 1) * ZSPAN, :] * weight_z, axis=0, keepdims=True)
            for c in range(3)
        ]
        speed = jnp.sqrt(sampled[0] * sampled[0] + sampled[1] * sampled[1] + sampled[2] * sampled[2])
        scale = -(strength * speed)
        spread = [weight_z * (scale * sampled[c]) for c in range(3)]
        spread = jnp.concatenate(spread + [jnp.zeros((8, 256), F32)], axis=0)
        rows_y = weight_y[out_first - first : out_first - first + out_span, :]
        patches.append(dot_over(rows_y, spread, ((1,), (1,))))
    for row in out_rows:
        where_at = pl.ds(row * CY + out_first - 8, out_span)
        value = total[where_at, :]
        for weight_x, patch in zip(weights_x, patches):
            value = value + weight_x[row + 5 : row + 6, :] * patch
        total[where_at, :] = value


def near_rim(block, low, high):
    hit = jnp.zeros((1, 128), F32)
    for half in range(2):
        pos_y, live = block[half : half + 1, :], block[4 + half : 5 + half, :] > 0.0
        hit = jnp.maximum(hit, (live & ((pos_y < low) | (pos_y > high))).astype(F32))
    return jnp.max(hit) > 0.0


def interior(
    vel, lm, mm, up, slab, points, xlow, xhigh, ulow, uhigh,
    lm_next, mm_next, visc, total, ev, ea, eu, xs, uh, mags,
):
    assemble(vel, lm, mm, slab, xlow, xhigh, ulow, uhigh, ev, ea, eu)
    closure_first(ev, xs, mags, (6, 14, 18))
    closure_hat(xs, uh, (7, 15, 17))
    closure_last(ea, up, xs, uh, mags, lm_next, mm_next, visc, (8, 16))
    total[...] = jnp.zeros((CX * CY, 128), F32)
    for dx, source, base in ((0, points, 0), (-1, xlow, 480), (1, xhigh, 480)):
        blocks = [source[pl.ds(base + t * 8, 8), :] for t in range(TURBINES)]
        turbines(blocks, dx, 0, eu, total, skip_rim=True)


def edges(
    up, points, xlow, xhigh, ylow, yhigh, lm_in, mm_in, visc_in, total_in, ev_in, ea_in, eu_in,
    lm_next, mm_next, visc, body, ev, ea, eu, xs, uh, mags, total,
):
    ev[...] = ev_in[...]
    ea[...] = ea_in[...]
    eu[...] = eu_in[...]
    total[...] = total_in[...]
    complete(ylow, yhigh, ev, ea, eu)
    for out, source in ((lm_next, lm_in), (mm_next, mm_in), (visc, visc_in)):
        for row in range(CX):
            out[pl.ds(row * CY + 8, 16), :] = source[pl.ds(row * CY + 8, 16), :]
    closure_first(ev, xs, mags, (-2, 4, 20, 26))
    closure_hat(xs, uh, (-1, 1, 23, 25))
    closure_last(ea, up, xs, uh, mags, lm_next, mm_next, visc, (0, 24))
    for dx, source, base in ((0, points, 0), (-1, xlow, 480), (1, xhigh, 480)):

        def column(t, carry, dx=dx, source=source, base=base):
            block = source[pl.ds(pl.multiple_of(base + t * 8, 8), 8), :]

            @pl.when(near_rim(block, 2.0, float(CY - 3)))
            def _():
                turbines([block], dx, 0, eu, total)

            return carry

        lax.fori_loop(0, TURBINES, column, 0)
    for dy, message in ((-1, ylow), (1, yhigh)):
        for k, dx in enumerate((0, -1, 1)):

            def rim(t, carry, dx=dx, dy=dy, message=message, k=k):
                block = message[pl.ds(pl.multiple_of(YP + k * 24 + t * 8, 8), 8), :]
                low, high = (-1.0, float(CY - 3)) if dy < 0 else (2.0, float(CY + 1))

                @pl.when(near_rim(block, low, high))
                def _():
                    turbines([block], dx, dy, eu, total)

                return carry

            lax.fori_loop(0, TURBINES, rim, 0)
    lane = lax.broadcasted_iota(jnp.int32, (CY, 128), 1)
    inside = (lane >= ZLOW) & (lane < ZLOW + ZSPAN)
    for row in range(CX):
        values = total[pl.ds(row * CY, CY), :]
        for c, shift in enumerate((ZLOW, NZ + ZLOW - ZSPAN, NZ + ZLOW - 2 * ZSPAN)):
            out = jnp.where(inside, pltpu.roll(values, shift % NZ, 1), 0.0)
            body[pl.ds((c * CX + row) * CY, CY), :] = out


VMEM = pl.BlockSpec(memory_space=pltpu.VMEM)


def rows(count):
    return jax.ShapeDtypeStruct((count, 128), F32)


def limit(mebibytes):
    return pltpu.CompilerParams(vmem_limit_bytes=mebibytes * 1024 * 1024)


def shards(velocity, lm_old, mm_old, upstream, point_pos, point_coef, tile_turbines):
    vel = velocity.reshape(3 * CX * CY, NZ)
    lm = lm_old.reshape(CX * CY, NZ)
    mm = mm_old.reshape(CX * CY, NZ)
    up = upstream.reshape(2 * CX * CY, NZ)
    low, high, slab, points = pl.pallas_call(
        pack_x,
        out_shape=(rows(XMSG), rows(XMSG), rows(CX * CY), rows(24)),
        in_specs=[VMEM] * 5 + [pl.BlockSpec(memory_space=pltpu.SMEM)],
        out_specs=(VMEM,) * 4,
        compiler_params=limit(8),
        name="pack_x",
    )(vel, lm, mm, point_pos.reshape(3, 1, TURBINES * SLOTS), point_coef[0], tile_turbines)
    xlow = shifted(high, "gx", 1)
    xhigh = shifted(low, "gx", -1)
    low, high, ulow, uhigh = pl.pallas_call(
        pack_y,
        out_shape=(rows(YMSG), rows(YMSG), rows(64), rows(64)),
        in_specs=[VMEM] * 7,
        out_specs=(VMEM,) * 4,
        compiler_params=limit(8),
        name="pack_y",
    )(vel, lm, mm, slab, points, xlow, xhigh)
    ylow = shifted(high, "gy", 1)
    yhigh = shifted(low, "gy", -1)
    scratch = [rows(3 * 12 * EY), rows(2 * 14 * EY), rows(18 * PY)]
    work = [pltpu.VMEM((n, 128), F32) for n in (15 * 10 * EY, 3 * 10 * EY, CX * EY)]
    first = pl.pallas_call(
        interior,
        out_shape=[rows(CX * CY)] * 4 + scratch,
        in_specs=[VMEM] * 10,
        out_specs=[VMEM] * 7,
        scratch_shapes=work,
        compiler_params=limit(16),
        cost_estimate=pl.CostEstimate(flops=20_000_000, bytes_accessed=20_000_000, transcendentals=0),
        name="interior",
    )(vel, lm, mm, up, slab, points, xlow, xhigh, ulow, uhigh)
    lm_next, mm_next, visc, body = pl.pallas_call(
        edges,
        out_shape=[rows(CX * CY)] * 3 + [rows(3 * CX * CY)],
        in_specs=[VMEM] * 13,
        out_specs=[VMEM] * 4,
        scratch_shapes=[pltpu.VMEM(s.shape, F32) for s in scratch]
        + work
        + [pltpu.VMEM((CX * CY, 128), F32)],
        compiler_params=limit(16),
        name="edges",
    )(up, points, xlow, xhigh, ylow, yhigh, *first)
    field = (CX, CY, NZ)
    return (
        lm_next.reshape(field),
        mm_next.reshape(field),
        visc.reshape(field),
        body.reshape(3, *field),
    )


def solution(mesh):
    return jax.shard_map(
        shards,
        mesh=mesh,
        in_specs=(
            P(None, "gx", "gy", None),
            P("gx", "gy", None),
            P("gx", "gy", None),
            P(None, "gx", "gy", None),
            P("gx", "gy", None, None),
            P("gx", "gy", None),
            P("gx", "gy"),
        ),
        out_specs=(
            P("gx", "gy", None),
            P("gx", "gy", None),
            P("gx", "gy", None),
            P(None, "gx", "gy", None),
        ),
        check_vma=False,
    )
```

```python
import math

import jax
import jax.numpy as jnp
from jax import lax
from jax.experimental import pallas as pl
from jax.experimental.pallas import tpu as pltpu
from jax.sharding import PartitionSpec as P

F32 = jnp.float32
CX, CY, NZ = 8, 32, 128
TURBINES, SLOTS = 3, 192
ZLOW, ZSPAN = 46, 40
XMSG = 504
YMSG = 320
YA, YU, YP = 72, 156, 248
EY = 40
PY = 48


def shifted(block, axis, distance):
    count = lax.axis_size(axis)
    return lax.ppermute(block, axis, [(i, (i + distance) % count) for i in range(count)])


def weight(offset):
    scaled = offset * (1.0 / 1.5)
    return jnp.maximum(jnp.exp(-(scaled * scaled)) - math.exp(-4.0), 0.0)


def packed(parts):
    lane = lax.broadcasted_iota(jnp.int32, parts[0].shape, 1)
    first = pltpu.roll(parts[0], NZ - ZLOW, 1)
    second = pltpu.roll(parts[1], NZ + ZSPAN - ZLOW, 1)
    third = pltpu.roll(parts[2], 2 * ZSPAN - ZLOW, 1)
    rest = jnp.where(lane < 3 * ZSPAN, third, 0.0)
    return jnp.where(lane < ZSPAN, first, jnp.where(lane < 2 * ZSPAN, second, rest))


def pack_x(vel_in, lm, mm, pos_in, coef_in, count, low, high, slab, points, vel, pos, coef, sems):
    span = 3 * CY
    copies = [
        (pos_in, pos),
        (coef_in, coef),
        (lm.at[pl.ds(0, span), :], low.at[pl.ds(192, span), :]),
        (mm.at[pl.ds(0, span), :], low.at[pl.ds(288, span), :]),
        (lm.at[pl.ds(5 * CY, span), :], high.at[pl.ds(192, span), :]),
        (mm.at[pl.ds(5 * CY, span), :], high.at[pl.ds(288, span), :]),
    ]
    copies += [
        (vel_in.at[pl.ds(c * 256, 256), :], vel.at[pl.ds(c * 256, 256), :]) for c in range(3)
    ]
    copies = [pltpu.make_async_copy(x, y, sems.at[i]) for i, (x, y) in enumerate(copies)]
    for copy in copies:
        copy.start()
    copies[0].wait()
    copies[1].wait()
    lane = lax.broadcasted_iota(jnp.int32, (1, 128), 1)
    turbine_count = count[0, 0]
    for t in range(TURBINES):
        lines = []
        for values in (pos[1], pos[2], coef[...]):
            lines.append(values[:, t * SLOTS : t * SLOTS + 128])
            lines.append(values[:, t * SLOTS + 64 : t * SLOTS + 192])
        live = jnp.where(t < turbine_count, 1.0, 0.0)
        lines[4] = lines[4] * live
        lines[5] = jnp.where(lane < 64, 0.0, lines[5] * live)
        lines.append(pos[0][:, t * SLOTS : t * SLOTS + 128])
        lines.append(jnp.zeros((1, 128), F32))
        block = jnp.concatenate(lines, axis=0)
        for out, base in ((low, 480), (high, 480), (points, 0)):
            out[pl.ds(base + 8 * t, 8), :] = block
    for copy in copies[6:]:
        copy.wait()
    for row in range(CX):
        parts = [vel[pl.ds((c * CX + row) * CY, CY), :] for c in range(3)]
        slab[pl.ds(row * CY, CY), :] = packed(parts)
    for out, first_v, first_u in ((low, 0, 2), (high, CX - 2, CX - 5)):
        for c in range(3):
            out[pl.ds(c * 64, 64), :] = vel[pl.ds((c * CX + first_v) * CY, 64), :]
        out[pl.ds(384, 96), :] = slab[pl.ds(first_u * CY, 96), :]
    for copy in copies[2:6]:
        copy.wait()


def pack_y(vel, lm, mm, slab, points, xlow, xhigh, low, high, ulow, uhigh):
    for out, message in ((ulow, xlow), (uhigh, xhigh)):
        for i in range(2):
            parts = [message[pl.ds(c * 64 + i * CY, CY), :] for c in range(3)]
            out[pl.ds(i * CY, CY), :] = packed(parts)
    for out, col_v, col_a, col_u in ((low, 0, 0, 0), (high, CY - 2, CY - 3, CY - 5)):
        for c in range(3):
            for j in range(2):
                base, col = (c * 2 + j) * 12, col_v + j
                out[pl.ds(base, 2), :] = xlow[pl.ds(c * 64 + col, 2, stride=CY), :]
                out[pl.ds(base + 2, 8), :] = vel[pl.ds(c * 256 + col, 8, stride=CY), :]
                out[pl.ds(base + 10, 2), :] = xhigh[pl.ds(c * 64 + col, 2, stride=CY), :]
        for f, own in enumerate((lm, mm)):
            for j in range(3):
                base, col = YA + (f * 3 + j) * 14, col_a + j
                out[pl.ds(base, 3), :] = xlow[pl.ds(192 + f * 96 + col, 3, stride=CY), :]
                out[pl.ds(base + 3, 8), :] = own[pl.ds(col, 8, stride=CY), :]
                out[pl.ds(base + 11, 3), :] = xhigh[pl.ds(192 + f * 96 + col, 3, stride=CY), :]
        for j in range(5):
            base, col = YU + j * 18, col_u + j
            out[pl.ds(base, 3), :] = xlow[pl.ds(384 + col, 3, stride=CY), :]
            out[pl.ds(base + 3, 2), :] = ulow[pl.ds(col, 2, stride=CY), :]
            out[pl.ds(base + 5, 8), :] = slab[pl.ds(col, 8, stride=CY), :]
            out[pl.ds(base + 13, 2), :] = uhigh[pl.ds(col, 2, stride=CY), :]
            out[pl.ds(base + 15, 3), :] = xhigh[pl.ds(384 + col, 3, stride=CY), :]
        out[pl.ds(YU + 90, 2), :] = jnp.zeros((2, 128), F32)
        for k, source in enumerate((points, xlow, xhigh)):
            first = 0 if k == 0 else 480
            out[pl.ds(YP + 24 * k, 24), :] = source[pl.ds(first, 24), :]


class Frame:
    def __init__(self, planes, width, turned):
        self.planes, self.width, self.turned = planes, width, turned

    def velocity(self, c, plane, cell):
        return (c * (self.planes + 4) + plane + 2) * self.width + cell + 4

    def average(self, f, plane, cell):
        return (f * (self.planes + 6) + plane + 3) * self.width + cell + 4

    def summed(self, q, plane, cell):
        return (q * (self.planes + 2) + plane + 1) * self.width + cell + 4

    def magnitude(self, plane, cell):
        return plane * self.width + cell + 4

    def sizes(self):
        n, w = self.planes, self.width
        return 3 * (n + 4) * w, 2 * (n + 6) * w, 15 * (n + 2) * w, 3 * (n + 2) * w, n * w


ROWS = Frame(CX, EY, False)
SIDE = Frame(3, 16, True)


def assemble(vel, lm, mm, slab, xlow, xhigh, ulow, uhigh, ev, ea, eu, tv, ta):
    for c in range(3):
        for row in range(CX):
            ev[pl.ds(ROWS.velocity(c, row, 0), CY), :] = vel[pl.ds((c * CX + row) * CY, CY), :]
        for i in range(2):
            ev[pl.ds(ROWS.velocity(c, i - 2, 0), CY), :] = xlow[pl.ds(c * 64 + i * CY, CY), :]
            ev[pl.ds(ROWS.velocity(c, i + 8, 0), CY), :] = xhigh[pl.ds(c * 64 + i * CY, CY), :]
    for f, own in enumerate((lm, mm)):
        for row in range(CX):
            ea[pl.ds(ROWS.average(f, row, 0), CY), :] = own[pl.ds(row * CY, CY), :]
        for i in range(3):
            source = 192 + f * 96 + i * CY
            ea[pl.ds(ROWS.average(f, i - 3, 0), CY), :] = xlow[pl.ds(source, CY), :]
            ea[pl.ds(ROWS.average(f, i + 8, 0), CY), :] = xhigh[pl.ds(source, CY), :]
    zero = jnp.zeros((8, 128), F32)
    for row in range(18):
        eu[pl.ds(row * PY, 8), :] = zero
        eu[pl.ds(row * PY + 40, 8), :] = zero
    for row in range(CX):
        eu[pl.ds((row + 5) * PY + 8, CY), :] = slab[pl.ds(row * CY, CY), :]
    for i in range(3):
        eu[pl.ds(i * PY + 8, CY), :] = xlow[pl.ds(384 + i * CY, CY), :]
        eu[pl.ds((i + 15) * PY + 8, CY), :] = xhigh[pl.ds(384 + i * CY, CY), :]
    for i in range(2):
        eu[pl.ds((i + 3) * PY + 8, CY), :] = ulow[pl.ds(i * CY, CY), :]
        eu[pl.ds((i + 13) * PY + 8, CY), :] = uhigh[pl.ds(i * CY, CY), :]
    size_v, size_a = SIDE.sizes()[:2]
    for side, first, planes in ((0, 0, range(0, 5)), (1, CY - 3, range(-2, 3))):
        for c in range(3):
            for plane in planes:
                source = ROWS.velocity(c, 0, first + plane)
                target = side * size_v + SIDE.velocity(c, plane, 0)
                for start, count in ((-2, 8), (6, 4)):
                    tv[pl.ds(target + start, count), :] = ev[
                        pl.ds(source + start * EY, count, stride=EY), :
                    ]
    for side, first, planes in ((0, 0, range(0, 6)), (1, CY - 3, range(-3, 3))):
        for f in range(2):
            for plane in planes:
                source = ROWS.average(f, 0, first + plane)
                target = side * size_a + SIDE.average(f, plane, 0)
                for start, count in ((-3, 8), (3, 8)):
                    ta[pl.ds(target + start, count), :] = ea[
                        pl.ds(source + start * EY, count, stride=EY), :
                    ]


def complete(ylow, yhigh, tv, ta, eu):
    size_v, size_a = SIDE.sizes()[:2]
    for side, message, plane_v, plane_a in ((0, ylow, -2, -3), (1, yhigh, 3, 3)):
        for c in range(3):
            for j in range(2):
                target = side * size_v + SIDE.velocity(c, plane_v + j, -2)
                tv[pl.ds(target, 12), :] = message[pl.ds((c * 2 + j) * 12, 12), :]
        for f in range(2):
            for j in range(3):
                target = side * size_a + SIDE.average(f, plane_a + j, -3)
                ta[pl.ds(target, 14), :] = message[pl.ds(YA + (f * 3 + j) * 14, 14), :]
    for message, first in ((ylow, 3), (yhigh, 40)):
        for j in range(5):
            for start, count in ((0, 8), (8, 8), (16, 2)):
                eu[pl.ds(start * PY + first + j, count, stride=PY), :] = message[
                    pl.ds(YU + j * 18 + start, count), :
                ]


PAIRS = ((0, 0), (1, 1), (2, 2), (0, 1), (0, 2), (1, 2))


def slope_z(values):
    lane = lax.broadcasted_iota(jnp.int32, values.shape, 1)
    above = jnp.where(lane == NZ - 1, values, pltpu.roll(values, NZ - 1, 1))
    below = jnp.where(lane == 0, values, pltpu.roll(values, 1, 1))
    return above - below


def tensor_of(slopes):
    parts = [slopes[0][0], slopes[1][1], slopes[2][2]]
    parts += [slopes[j][i] + slopes[i][j] for i, j in PAIRS[3:]]
    diag = parts[0] * parts[0] + parts[1] * parts[1] + parts[2] * parts[2]
    off = parts[3] * parts[3] + parts[4] * parts[4] + parts[5] * parts[5]
    return parts, jnp.sqrt(2.0 * diag + off)


def closure_first(frame, ev, xs, mags, starts):
    def at(c, plane, cell):
        return ev[pl.ds(frame.velocity(c, plane, cell), 8), :]

    def put(q, plane, cell, value):
        xs[pl.ds(frame.summed(q, plane, cell), 8), :] = value

    for cell in starts:
        before = [at(c, -2, cell) for c in range(3)]
        here = [at(c, -1, cell) for c in range(3)]
        history = []
        for plane in range(-1, frame.planes + 1):
            after = [at(c, plane + 1, cell) for c in range(3)]
            slopes = [
                [after[c] - before[c] for c in range(3)],
                [at(c, plane, cell + 1) - at(c, plane, cell - 1) for c in range(3)],
            ]
            if frame.turned:
                slopes.reverse()
            slopes.append([slope_z(here[c]) for c in range(3)])
            parts, mag = tensor_of(slopes)
            now = [mag * part for part in parts] + [here[i] * here[j] for i, j in PAIRS]
            if 0 <= plane < frame.planes:
                mags[pl.ds(frame.magnitude(plane, cell), 8), :] = mag
            for c in range(3):
                put(12 + c, plane, cell, before[c] + (here[c] + here[c]) + after[c])
            history.append(now)
            if len(history) == 3:
                for q in range(12):
                    value = history[0][q] + (history[1][q] + history[1][q]) + history[2][q]
                    put(q, plane - 1, cell, value)
                history.pop(0)
            before, here = here, after


def closure_hat(frame, xs, uh, starts):
    for c in range(3):
        for plane in range(-1, frame.planes + 1):
            for cell in starts:
                base = frame.summed(12 + c, plane, cell)
                mid = xs[pl.ds(base, 8), :]
                value = xs[pl.ds(base - 1, 8), :] + (mid + mid) + xs[pl.ds(base + 1, 8), :]
                uh[pl.ds(frame.summed(c, plane, cell), 8), :] = value


def take_rows(values, index):
    return jnp.take_along_axis(values, index, axis=0)


def averages_up(frame, ea, shift_plane, shift_cell, plane, cell):
    sub = lax.broadcasted_iota(jnp.int32, (8, 128), 0)
    index = sub - shift_cell + 3
    early = index < 8
    first = jnp.minimum(index, 7)
    second = jnp.maximum(index - 6, 0)
    result = [None, None]
    for shift in range(-3, 4):
        chosen = shift_plane == shift
        for f in range(2):
            base = frame.average(f, plane - shift, cell)
            value = jnp.where(
                early,
                take_rows(ea[pl.ds(base - 3, 8), :], first),
                take_rows(ea[pl.ds(base + 3, 8), :], second),
            )
            result[f] = value if result[f] is None else jnp.where(chosen, value, result[f])
    return result


def closure_last(frame, ea, up, xs, uh, mags, outs, starts, first=0):
    def summed(q, plane, cell):
        base = frame.summed(q, plane, cell)
        mid = xs[pl.ds(base, 8), :]
        return xs[pl.ds(base - 1, 8), :] + (mid + mid) + xs[pl.ds(base + 1, 8), :]

    def hat(c, plane, cell):
        return uh[pl.ds(frame.summed(c, plane, cell), 8), :]

    for plane in range(frame.planes):
        for cell in starts:
            here = [hat(c, plane, cell) for c in range(3)]
            slopes = [
                [hat(c, plane + 1, cell) - hat(c, plane - 1, cell) for c in range(3)],
                [hat(c, plane, cell + 1) - hat(c, plane, cell - 1) for c in range(3)],
            ]
            shifts = [
                pl.ds(d * CX * CY + plane * CY + cell, 8)
                if not frame.turned
                else pl.ds(d * CX * CY + cell * CY + first + plane, 8, stride=CY)
                for d in range(2)
            ]
            if frame.turned:
                slopes.reverse()
                shifts.reverse()
            slopes.append([slope_z(here[c]) for c in range(3)])
            parts, mag = tensor_of(slopes)
            mag = 0.25 * mag
            lm_sum = diag = off = None
            for q, (i, j) in enumerate(PAIRS):
                model = summed(q, plane, cell) - mag * parts[q]
                leonard = summed(6 + q, plane, cell) - (1.0 / 16.0) * (here[i] * here[j])
                term = leonard * model
                lm_sum = term if lm_sum is None else lm_sum + term
                square = model * model
                if q < 3:
                    diag = square if diag is None else diag + square
                else:
                    off = square if off is None else off + square
            lm_term = lm_sum * (1.0 / 512.0)
            mm_term = (2.0 * diag + off) * (1.0 / 2048.0)
            lm_up, mm_up = averages_up(frame, ea, up[shifts[0], :], up[shifts[1], :], plane, cell)
            ratio = (0.2 / 1.5) * jnp.sqrt(jnp.sqrt(jnp.sqrt(lm_up * mm_up)))
            inverse = 1.0 / (1.0 + ratio)
            lm_new = jnp.maximum((ratio * lm_term + lm_up) * inverse, 0.0)
            mm_new = (ratio * mm_term + mm_up) * inverse
            smag = 0.5 * mags[pl.ds(frame.magnitude(plane, cell), 8), :]
            if frame.turned:
                where_at = pl.ds(cell * CY + first + plane, 8, stride=CY)
            else:
                where_at = pl.ds(plane * CY + cell, 8)
            for out, value in zip(outs, (lm_new, mm_new, lm_new / mm_new * smag)):
                out[where_at, :] = value


def split(values):
    high = values.astype(jnp.bfloat16)
    return high, (values - high.astype(F32)).astype(jnp.bfloat16)


def dot_over(a, b, dims):
    (a_high, a_low), (b_high, b_low) = split(a), split(b)

    def dot(x, y):
        return lax.dot_general(x, y, (dims, ((), ())), preferred_element_type=F32)

    return dot(a_high, b_high) + dot(a_high, b_low) + dot(a_low, b_high)


def near_rim(pos_y, strength):
    return (strength > 0.0) & ((pos_y < 2.0) | (pos_y > float(CY - 3)))


def turbines(blocks, shift_x, shift_y, in_rows, first, span, out_rows, out_at, eu, total, rim=None):
    begin, stride, columns_out = out_at
    cell_x = lax.broadcasted_iota(jnp.int32, (24, 128), 0).astype(F32) - 5.0 - shift_x
    cell_y = lax.broadcasted_iota(jnp.int32, (span, 256), 0).astype(F32) + shift_y
    cell_z = lax.broadcasted_iota(jnp.int32, (ZSPAN, 256), 0).astype(F32) + float(ZLOW)
    weights_x = [weight(cell_x - block[6:7, :]) for block in blocks]
    planes = [None] * len(blocks)
    for row in in_rows:
        values = eu[pl.ds((row + 5) * PY + first, span), :]
        for t, weight_x in enumerate(weights_x):
            term = weight_x[row + 5 : row + 6, :] * values
            planes[t] = term if planes[t] is None else planes[t] + term
    patches = []
    for block, plane in zip(blocks, planes):
        pos_y = jnp.concatenate([block[0:1, :], block[1:2, :]], axis=1)
        pos_z = jnp.concatenate([block[2:3, :], block[3:4, :]], axis=1)
        strength = jnp.concatenate([block[4:5, :], block[5:6, :]], axis=1)
        if rim is not None:
            hit = jnp.max(near_rim(pos_y, strength).astype(F32), axis=1, keepdims=True)
            strength = strength * (hit if rim else 1.0 - hit)
        weight_y = weight(cell_y - pos_y)
        weight_z = weight(cell_z - pos_z)
        columns = dot_over(plane.T, weight_y, ((1,), (0,)))
        sampled = [
            jnp.sum(columns[c * ZSPAN : (c + 1) * ZSPAN, :] * weight_z, axis=0, keepdims=True)
            for c in range(3)
        ]
        speed = jnp.sqrt(sampled[0] * sampled[0] + sampled[1] * sampled[1] + sampled[2] * sampled[2])
        scale = -(strength * speed)
        spread = [weight_z * (scale * sampled[c]) for c in range(3)]
        spread = jnp.concatenate(spread + [jnp.zeros((8, 256), F32)], axis=0)
        rows_y = weight_y[8 : 8 + CY, :] if columns_out == CY else weight_y
        patches.append(dot_over(rows_y, spread, ((1,), (1,))))
    for row in out_rows:
        where_at = pl.ds(row * stride + begin, columns_out)
        value = total[where_at, :]
        for weight_x, patch in zip(weights_x, patches):
            value = value + weight_x[row + 5 : row + 6, :] * patch
        total[where_at, :] = value


def interior(
    vel, lm, mm, up, slab, points, xlow, xhigh, ulow, uhigh,
    lm_next, mm_next, visc, total, eu, tv, ta, ev, ea, xs, uh, mags,
):
    assemble(vel, lm, mm, slab, xlow, xhigh, ulow, uhigh, ev, ea, eu, tv, ta)
    closure_first(ROWS, ev, xs, mags, (1, 9, 17, 23))
    closure_hat(ROWS, xs, uh, (2, 10, 18, 22))
    closure_last(ROWS, ea, up, xs, uh, mags, (lm_next, mm_next, visc), (3, 11, 19, 21))
    total[...] = jnp.zeros((CX * CY, 128), F32)
    for source, base, shift_x, in_rows, out_rows in (
        (points, 0, 0.0, range(-2, 11), range(0, 8)),
        (xlow, 480, -8.0, range(-5, 3), range(0, 3)),
        (xhigh, 480, 8.0, range(6, 13), range(6, 8)),
    ):
        blocks = [source[pl.ds(base + t * 8, 8), :] for t in range(TURBINES)]
        turbines(blocks, shift_x, -8.0, in_rows, 0, PY, out_rows, (0, CY, CY), eu, total, rim=False)


def group_hits(everyone):
    lines = []
    for g in range(9):

        def line(q):
            return everyone[pl.ds(g * 24 + q, TURBINES, stride=8), :]

        reach_x = {0: None, 1: line(6) > 5.0, 2: line(6) < 2.0}[g % 3]
        hit = None
        for half in range(2):
            pos_y, strength = line(half), line(4 + half)
            if g < 3:
                found = near_rim(pos_y, strength)
            elif g < 6:
                found = (strength > 0.0) & (pos_y > float(CY - 3))
            else:
                found = (strength > 0.0) & (pos_y < 2.0)
            if reach_x is not None:
                found = found & reach_x
            hit = found if hit is None else hit | found
        lines.append(jnp.max(hit.astype(F32), axis=0, keepdims=True) * float(2**g))
    lines = jnp.concatenate(lines, axis=0)
    return jnp.sum(jnp.max(lines, axis=1, keepdims=True)).astype(jnp.int32)


def edges(
    up, points, xlow, xhigh, ylow, yhigh, lm_in, mm_in, visc_in, total_in, eu_in, tv_in, ta_in,
    lm_next, mm_next, visc, body, tv, ta, eu, xs, uh, mags, total, everyone, results, forces, sems,
):
    everyone[pl.ds(0, 24), :] = points[...]
    everyone[pl.ds(24, 24), :] = xlow[pl.ds(480, 24), :]
    everyone[pl.ds(48, 24), :] = xhigh[pl.ds(480, 24), :]
    everyone[pl.ds(72, 72), :] = ylow[pl.ds(YP, 72), :]
    everyone[pl.ds(144, 72), :] = yhigh[pl.ds(YP, 72), :]
    hits = group_hits(everyone)
    tv[...] = tv_in[...]
    ta[...] = ta_in[...]
    eu[...] = eu_in[...]
    for row in range(CX):
        total[pl.ds(row * PY + 8, CY), :] = total_in[pl.ds(row * CY, CY), :]
    complete(ylow, yhigh, tv, ta, eu)
    outs = [results.at[pl.ds(i * CX * CY, CX * CY), :] for i in range(3)]
    for out, source in zip(outs, (lm_in, mm_in, visc_in)):
        out[...] = source[...]
    size_v, size_a = SIDE.sizes()[:2]
    for side, first in ((0, 0), (1, CY - 3)):
        velocity = tv.at[pl.ds(side * size_v, size_v), :]
        averages = ta.at[pl.ds(side * size_a, size_a), :]
        closure_first(SIDE, velocity, xs, mags, (-2, 2))
        closure_hat(SIDE, xs, uh, (-1, 1))
        closure_last(SIDE, averages, up, xs, uh, mags, outs, (0,), first)
    copies = [
        pltpu.make_async_copy(out, target, sems.at[i])
        for i, (out, target) in enumerate(zip(outs, (lm_next, mm_next, visc)))
    ]
    for copy in copies:
        copy.start()

    def group(g):
        blocks = [everyone[pl.ds(pl.multiple_of(g * 24 + t * 8, 8), 8), :] for t in range(TURBINES)]
        k = lax.rem(g, 3)
        shift_x = jnp.where(k == 0, 0.0, jnp.where(k == 1, -8.0, 8.0))
        return blocks, shift_x

    def column(g, carry):
        @pl.when(lax.rem(lax.shift_right_logical(hits, g), 2) == 1)
        def _():
            blocks, shift_x = group(g)
            turbines(
                blocks, shift_x, -8.0, range(-5, 13), 0, PY, range(0, 8), (8, PY, CY), eu, total, rim=True
            )

        return carry

    def beyond(g, carry):
        @pl.when(lax.rem(lax.shift_right_logical(hits, g), 2) == 1)
        def _():
            blocks, shift_x = group(g)
            above = g >= 6
            first = pl.multiple_of(jnp.where(above, 32, 0), 8)
            shift_y = jnp.where(above, -8.0, 24.0)
            turbines(
                blocks, shift_x, shift_y, range(-5, 13), first, 16, range(0, 8), (first, PY, 16), eu, total
            )

        return carry

    lax.fori_loop(0, 3, column, 0)
    lax.fori_loop(3, 9, beyond, 0)
    lane = lax.broadcasted_iota(jnp.int32, (CY, 128), 1)
    inside = (lane >= ZLOW) & (lane < ZLOW + ZSPAN)
    for row in range(CX):
        values = total[pl.ds(row * PY + 8, CY), :]
        for c, shift in enumerate((ZLOW, NZ + ZLOW - ZSPAN, NZ + ZLOW - 2 * ZSPAN)):
            out = jnp.where(inside, pltpu.roll(values, shift % NZ, 1), 0.0)
            forces[pl.ds((c * CX + row) * CY, CY), :] = out
        if row % 4 == 3:
            for c in range(3):
                part = pl.ds((c * CX + row - 3) * CY, 4 * CY)
                copy = pltpu.make_async_copy(
                    forces.at[part, :], body.at[part, :], sems.at[len(copies)]
                )
                copy.start()
                copies.append(copy)
    for copy in copies:
        copy.wait()


VMEM = pl.BlockSpec(memory_space=pltpu.VMEM)
HBM = pl.BlockSpec(memory_space=pltpu.HBM)


def rows(count):
    return jax.ShapeDtypeStruct((count, 128), F32)


def limit(mebibytes):
    return pltpu.CompilerParams(vmem_limit_bytes=mebibytes * 1024 * 1024)


def shards(velocity, lm_old, mm_old, upstream, point_pos, point_coef, tile_turbines):
    vel = velocity.reshape(3 * CX * CY, NZ)
    lm = lm_old.reshape(CX * CY, NZ)
    mm = mm_old.reshape(CX * CY, NZ)
    up = upstream.reshape(2 * CX * CY, NZ)
    low, high, slab, points = pl.pallas_call(
        pack_x,
        out_shape=(rows(XMSG), rows(XMSG), rows(CX * CY), rows(24)),
        in_specs=[HBM] * 5 + [pl.BlockSpec(memory_space=pltpu.SMEM)],
        out_specs=(VMEM,) * 4,
        scratch_shapes=[
            pltpu.VMEM((3 * CX * CY, 128), F32),
            pltpu.VMEM((3, 1, TURBINES * SLOTS), F32),
            pltpu.VMEM((1, TURBINES * SLOTS), F32),
            pltpu.SemaphoreType.DMA((9,)),
        ],
        compiler_params=limit(8),
        name="pack_x",
    )(
        *(
            pltpu.with_memory_space_constraint(value, pltpu.HBM)
            for value in (vel, lm, mm, point_pos.reshape(3, 1, TURBINES * SLOTS), point_coef[0])
        ),
        tile_turbines,
    )
    xlow = shifted(high, "gx", 1)
    xhigh = shifted(low, "gx", -1)
    low, high, ulow, uhigh = pl.pallas_call(
        pack_y,
        out_shape=(rows(YMSG), rows(YMSG), rows(64), rows(64)),
        in_specs=[VMEM] * 7,
        out_specs=(VMEM,) * 4,
        compiler_params=limit(8),
        name="pack_y",
    )(vel, lm, mm, slab, points, xlow, xhigh)
    ylow = shifted(high, "gy", 1)
    yhigh = shifted(low, "gy", -1)
    size_v, size_a = SIDE.sizes()[:2]
    handed = [18 * PY, 2 * size_v, 2 * size_a]
    first = pl.pallas_call(
        interior,
        out_shape=[rows(CX * CY)] * 4 + [rows(n) for n in handed],
        in_specs=[VMEM] * 10,
        out_specs=[VMEM] * 7,
        scratch_shapes=[pltpu.VMEM((n, 128), F32) for n in ROWS.sizes()],
        compiler_params=limit(16),
        cost_estimate=pl.CostEstimate(flops=20_000_000, bytes_accessed=20_000_000, transcendentals=0),
        name="interior",
    )(vel, lm, mm, up, slab, points, xlow, xhigh, ulow, uhigh)
    eu, tv, ta = handed
    own = [tv, ta, eu, *SIDE.sizes()[2:], CX * PY, 9 * 24, 3 * CX * CY, 3 * CX * CY]
    lm_next, mm_next, visc, body = pl.pallas_call(
        edges,
        out_shape=[rows(CX * CY)] * 3 + [rows(3 * CX * CY)],
        in_specs=[VMEM] * 13,
        out_specs=[HBM] * 4,
        scratch_shapes=[pltpu.VMEM((n, 128), F32) for n in own] + [pltpu.SemaphoreType.DMA((9,))],
        compiler_params=limit(16),
        name="edges",
    )(up, points, xlow, xhigh, ylow, yhigh, *first)
    field = (CX, CY, NZ)
    return (
        lm_next.reshape(field),
        mm_next.reshape(field),
        visc.reshape(field),
        body.reshape(3, *field),
    )


def solution(mesh):
    return jax.shard_map(
        shards,
        mesh=mesh,
        in_specs=(
            P(None, "gx", "gy", None),
            P("gx", "gy", None),
            P("gx", "gy", None),
            P(None, "gx", "gy", None),
            P("gx", "gy", None, None),
            P("gx", "gy", None),
            P("gx", "gy"),
        ),
        out_specs=(
            P("gx", "gy", None),
            P("gx", "gy", None),
            P("gx", "gy", None),
            P(None, "gx", "gy", None),
        ),
        check_vma=False,
    )
```

```python
import math

import jax
import jax.numpy as jnp
from jax import lax
from jax.experimental import pallas as pl
from jax.experimental.pallas import tpu as pltpu
from jax.sharding import PartitionSpec as P

F32 = jnp.float32
CX, CY, NZ = 8, 32, 128
TURBINES, SLOTS = 3, 192
ZLOW, ZSPAN = 46, 40
XMSG = 504
YMSG = 320
YA, YU, YP = 72, 156, 248
EY = 40
PY = 48


def shifted(block, axis, distance):
    count = lax.axis_size(axis)
    return lax.ppermute(block, axis, [(i, (i + distance) % count) for i in range(count)])


def weight(offset):
    scaled = offset * (1.0 / 1.5)
    return jnp.maximum(jnp.exp(-(scaled * scaled)) - math.exp(-4.0), 0.0)


def packed(parts):
    lane = lax.broadcasted_iota(jnp.int32, parts[0].shape, 1)
    first = pltpu.roll(parts[0], NZ - ZLOW, 1)
    second = pltpu.roll(parts[1], NZ + ZSPAN - ZLOW, 1)
    third = pltpu.roll(parts[2], 2 * ZSPAN - ZLOW, 1)
    rest = jnp.where(lane < 3 * ZSPAN, third, 0.0)
    return jnp.where(lane < ZSPAN, first, jnp.where(lane < 2 * ZSPAN, second, rest))


def pack_x(
    vel_in, lm_in, mm_in, pos_in, coef_in, count_in,
    low, high, slab, points, vel, lm, mm, pos, coef, count, sems,
):
    pairs = (
        (vel_in, vel), (pos_in, pos), (coef_in, coef), (count_in, count), (lm_in, lm), (mm_in, mm),
    )
    copies = [pltpu.make_async_copy(x, y, sems.at[i]) for i, (x, y) in enumerate(pairs)]
    for copy in copies:
        copy.start()
    for copy in copies[1:4]:
        copy.wait()
    lane = lax.broadcasted_iota(jnp.int32, (1, 128), 1)
    turbine_count = jnp.broadcast_to(count[...], (1, 128))
    for t in range(TURBINES):
        lines = []
        for values in (pos[1], pos[2], coef[...]):
            lines.append(values[:, t * SLOTS : t * SLOTS + 128])
            lines.append(values[:, t * SLOTS + 64 : t * SLOTS + 192])
        live = turbine_count > t
        lines[4] = jnp.where(live, lines[4], 0.0)
        lines[5] = jnp.where(live & (lane >= 64), lines[5], 0.0)
        lines.append(pos[0][:, t * SLOTS : t * SLOTS + 128])
        lines.append(jnp.zeros((1, 128), F32))
        block = jnp.concatenate(lines, axis=0)
        for out, base in ((low, 480), (high, 480), (points, 0)):
            out[pl.ds(base + 8 * t, 8), :] = block
    copies[0].wait()
    for row in range(CX):
        parts = [vel[pl.ds((c * CX + row) * CY, CY), :] for c in range(3)]
        value = packed(parts)
        slab[pl.ds(row * CY, CY), :] = value
        if 2 <= row < 5:
            low[pl.ds(384 + (row - 2) * CY, CY), :] = value
        if 3 <= row < 6:
            high[pl.ds(384 + (row - 3) * CY, CY), :] = value
        for out, first in ((low, 0), (high, CX - 2)):
            if first <= row < first + 2:
                for c in range(3):
                    out[pl.ds(c * 64 + (row - first) * CY, CY), :] = parts[c]
    copies[4].wait()
    copies[5].wait()
    for out, first in ((low, 0), (high, CX - 3)):
        for f, own in enumerate((lm, mm)):
            out[pl.ds(192 + f * 96, 96), :] = own[pl.ds(first * CY, 96), :]


def pack_y(vel, lm, mm, slab, points, xlow, xhigh, low, high, ulow, uhigh):
    for out, message in ((ulow, xlow), (uhigh, xhigh)):
        for i in range(2):
            parts = [message[pl.ds(c * 64 + i * CY, CY), :] for c in range(3)]
            out[pl.ds(i * CY, CY), :] = packed(parts)
    for out, col_v, col_a, col_u in ((low, 0, 0, 0), (high, CY - 2, CY - 3, CY - 5)):
        for c in range(3):
            for j in range(2):
                base, col = (c * 2 + j) * 12, col_v + j
                out[pl.ds(base, 2), :] = xlow[pl.ds(c * 64 + col, 2, stride=CY), :]
                out[pl.ds(base + 2, 8), :] = vel[pl.ds(c * 256 + col, 8, stride=CY), :]
                out[pl.ds(base + 10, 2), :] = xhigh[pl.ds(c * 64 + col, 2, stride=CY), :]
        for f, own in enumerate((lm, mm)):
            for j in range(3):
                base, col = YA + (f * 3 + j) * 14, col_a + j
                out[pl.ds(base, 3), :] = xlow[pl.ds(192 + f * 96 + col, 3, stride=CY), :]
                out[pl.ds(base + 3, 8), :] = own[pl.ds(col, 8, stride=CY), :]
                out[pl.ds(base + 11, 3), :] = xhigh[pl.ds(192 + f * 96 + col, 3, stride=CY), :]
        for j in range(5):
            base, col = YU + j * 18, col_u + j
            out[pl.ds(base, 3), :] = xlow[pl.ds(384 + col, 3, stride=CY), :]
            out[pl.ds(base + 3, 2), :] = ulow[pl.ds(col, 2, stride=CY), :]
            out[pl.ds(base + 5, 8), :] = slab[pl.ds(col, 8, stride=CY), :]
            out[pl.ds(base + 13, 2), :] = uhigh[pl.ds(col, 2, stride=CY), :]
            out[pl.ds(base + 15, 3), :] = xhigh[pl.ds(384 + col, 3, stride=CY), :]
        out[pl.ds(YU + 90, 2), :] = jnp.zeros((2, 128), F32)
        for k, source in enumerate((points, xlow, xhigh)):
            first = 0 if k == 0 else 480
            out[pl.ds(YP + 24 * k, 24), :] = source[pl.ds(first, 24), :]


class Frame:
    def __init__(self, planes, width, turned):
        self.planes, self.width, self.turned = planes, width, turned

    def velocity(self, c, plane, cell):
        return (c * (self.planes + 4) + plane + 2) * self.width + cell + 4

    def average(self, f, plane, cell):
        return (f * (self.planes + 6) + plane + 3) * self.width + cell + 4

    def summed(self, q, plane, cell):
        return (q * (self.planes + 2) + plane + 1) * self.width + cell + 4

    def magnitude(self, plane, cell):
        return plane * self.width + cell + 4

    def sizes(self):
        n, w = self.planes, self.width
        return 3 * (n + 4) * w, 2 * (n + 6) * w, 15 * (n + 2) * w, 3 * (n + 2) * w, n * w


ROWS = Frame(CX, EY, False)
SIDE = Frame(3, 16, True)


def assemble(vel, lm, mm, slab, xlow, xhigh, ulow, uhigh, ev, ea, eu, tv, ta):
    for c in range(3):
        for row in range(CX):
            ev[pl.ds(ROWS.velocity(c, row, 0), CY), :] = vel[pl.ds((c * CX + row) * CY, CY), :]
        for i in range(2):
            ev[pl.ds(ROWS.velocity(c, i - 2, 0), CY), :] = xlow[pl.ds(c * 64 + i * CY, CY), :]
            ev[pl.ds(ROWS.velocity(c, i + 8, 0), CY), :] = xhigh[pl.ds(c * 64 + i * CY, CY), :]
    for f, own in enumerate((lm, mm)):
        for row in range(CX):
            ea[pl.ds(ROWS.average(f, row, 0), CY), :] = own[pl.ds(row * CY, CY), :]
        for i in range(3):
            source = 192 + f * 96 + i * CY
            ea[pl.ds(ROWS.average(f, i - 3, 0), CY), :] = xlow[pl.ds(source, CY), :]
            ea[pl.ds(ROWS.average(f, i + 8, 0), CY), :] = xhigh[pl.ds(source, CY), :]
    zero = jnp.zeros((8, 128), F32)
    for row in range(18):
        eu[pl.ds(row * PY, 8), :] = zero
        eu[pl.ds(row * PY + 40, 8), :] = zero
    for row in range(CX):
        eu[pl.ds((row + 5) * PY + 8, CY), :] = slab[pl.ds(row * CY, CY), :]
    for i in range(3):
        eu[pl.ds(i * PY + 8, CY), :] = xlow[pl.ds(384 + i * CY, CY), :]
        eu[pl.ds((i + 15) * PY + 8, CY), :] = xhigh[pl.ds(384 + i * CY, CY), :]
    for i in range(2):
        eu[pl.ds((i + 3) * PY + 8, CY), :] = ulow[pl.ds(i * CY, CY), :]
        eu[pl.ds((i + 13) * PY + 8, CY), :] = uhigh[pl.ds(i * CY, CY), :]
    size_v, size_a = SIDE.sizes()[:2]
    for side, first, planes in ((0, 0, range(0, 5)), (1, CY - 3, range(-2, 3))):
        for c in range(3):
            for plane in planes:
                source = ROWS.velocity(c, 0, first + plane)
                target = side * size_v + SIDE.velocity(c, plane, 0)
                for start, count in ((-2, 8), (6, 4)):
                    tv[pl.ds(target + start, count), :] = ev[
                        pl.ds(source + start * EY, count, stride=EY), :
                    ]
    for side, first, planes in ((0, 0, range(0, 6)), (1, CY - 3, range(-3, 3))):
        for f in range(2):
            for plane in planes:
                source = ROWS.average(f, 0, first + plane)
                target = side * size_a + SIDE.average(f, plane, 0)
                for start, count in ((-3, 8), (3, 8)):
                    ta[pl.ds(target + start, count), :] = ea[
                        pl.ds(source + start * EY, count, stride=EY), :
                    ]


def complete(ylow, yhigh, tv, ta, eu):
    size_v, size_a = SIDE.sizes()[:2]
    for side, message, plane_v, plane_a in ((0, ylow, -2, -3), (1, yhigh, 3, 3)):
        for c in range(3):
            for j in range(2):
                target = side * size_v + SIDE.velocity(c, plane_v + j, -2)
                tv[pl.ds(target, 12), :] = message[pl.ds((c * 2 + j) * 12, 12), :]
        for f in range(2):
            for j in range(3):
                target = side * size_a + SIDE.average(f, plane_a + j, -3)
                ta[pl.ds(target, 14), :] = message[pl.ds(YA + (f * 3 + j) * 14, 14), :]
    for message, first in ((ylow, 3), (yhigh, 40)):
        for j in range(5):
            for start, count in ((0, 8), (8, 8), (16, 2)):
                eu[pl.ds(start * PY + first + j, count, stride=PY), :] = message[
                    pl.ds(YU + j * 18 + start, count), :
                ]


PAIRS = ((0, 0), (1, 1), (2, 2), (0, 1), (0, 2), (1, 2))


def slope_z(values):
    lane = lax.broadcasted_iota(jnp.int32, values.shape, 1)
    above = jnp.where(lane == NZ - 1, values, pltpu.roll(values, NZ - 1, 1))
    below = jnp.where(lane == 0, values, pltpu.roll(values, 1, 1))
    return above - below


def tensor_of(slopes):
    parts = [slopes[0][0], slopes[1][1], slopes[2][2]]
    parts += [slopes[j][i] + slopes[i][j] for i, j in PAIRS[3:]]
    diag = parts[0] * parts[0] + parts[1] * parts[1] + parts[2] * parts[2]
    off = parts[3] * parts[3] + parts[4] * parts[4] + parts[5] * parts[5]
    return parts, jnp.sqrt(2.0 * diag + off)


def closure_first(frame, ev, xs, mags, starts):
    def at(c, plane, cell):
        return ev[pl.ds(frame.velocity(c, plane, cell), 8), :]

    def put(q, plane, cell, value):
        xs[pl.ds(frame.summed(q, plane, cell), 8), :] = value

    for cell in starts:
        before = [at(c, -2, cell) for c in range(3)]
        here = [at(c, -1, cell) for c in range(3)]
        history = []
        for plane in range(-1, frame.planes + 1):
            after = [at(c, plane + 1, cell) for c in range(3)]
            slopes = [
                [after[c] - before[c] for c in range(3)],
                [at(c, plane, cell + 1) - at(c, plane, cell - 1) for c in range(3)],
            ]
            if frame.turned:
                slopes.reverse()
            slopes.append([slope_z(here[c]) for c in range(3)])
            parts, mag = tensor_of(slopes)
            now = [mag * part for part in parts] + [here[i] * here[j] for i, j in PAIRS]
            if 0 <= plane < frame.planes:
                mags[pl.ds(frame.magnitude(plane, cell), 8), :] = mag
            for c in range(3):
                put(12 + c, plane, cell, before[c] + (here[c] + here[c]) + after[c])
            history.append(now)
            if len(history) == 3:
                for q in range(12):
                    value = history[0][q] + (history[1][q] + history[1][q]) + history[2][q]
                    put(q, plane - 1, cell, value)
                history.pop(0)
            before, here = here, after


def closure_hat(frame, xs, uh, starts):
    for c in range(3):
        for plane in range(-1, frame.planes + 1):
            for cell in starts:
                base = frame.summed(12 + c, plane, cell)
                mid = xs[pl.ds(base, 8), :]
                value = xs[pl.ds(base - 1, 8), :] + (mid + mid) + xs[pl.ds(base + 1, 8), :]
                uh[pl.ds(frame.summed(c, plane, cell), 8), :] = value


def take_rows(values, index):
    return jnp.take_along_axis(values, index, axis=0)


def averages_up(frame, ea, shift_plane, shift_cell, plane, cell):
    sub = lax.broadcasted_iota(jnp.int32, (8, 128), 0)
    index = sub - shift_cell + 3
    early = index < 8
    first = jnp.minimum(index, 7)
    second = jnp.maximum(index - 6, 0)
    result = [None, None]
    for shift in range(-3, 4):
        chosen = shift_plane == shift
        for f in range(2):
            base = frame.average(f, plane - shift, cell)
            value = jnp.where(
                early,
                take_rows(ea[pl.ds(base - 3, 8), :], first),
                take_rows(ea[pl.ds(base + 3, 8), :], second),
            )
            result[f] = value if result[f] is None else jnp.where(chosen, value, result[f])
    return result


def closure_last(frame, ea, up, xs, uh, mags, outs, starts, first=0, skipped=0):
    def summed(q, plane, cell):
        base = frame.summed(q, plane, cell)
        mid = xs[pl.ds(base, 8), :]
        return xs[pl.ds(base - 1, 8), :] + (mid + mid) + xs[pl.ds(base + 1, 8), :]

    def hat(c, plane, cell):
        return uh[pl.ds(frame.summed(c, plane, cell), 8), :]

    for plane in range(frame.planes):
        for cell in starts:
            here = [hat(c, plane, cell) for c in range(3)]
            slopes = [
                [hat(c, plane + 1, cell) - hat(c, plane - 1, cell) for c in range(3)],
                [hat(c, plane, cell + 1) - hat(c, plane, cell - 1) for c in range(3)],
            ]
            shifts = [
                pl.ds(d * CX * CY + plane * CY + cell, 8)
                if not frame.turned
                else pl.ds(d * CX * CY + cell * CY + first + plane, 8, stride=CY)
                for d in range(2)
            ]
            if frame.turned:
                slopes.reverse()
                shifts.reverse()
            slopes.append([slope_z(here[c]) for c in range(3)])
            parts, mag = tensor_of(slopes)
            mag = 0.25 * mag
            lm_sum = diag = off = None
            for q, (i, j) in enumerate(PAIRS):
                model = summed(q, plane, cell) - mag * parts[q]
                leonard = summed(6 + q, plane, cell) - (1.0 / 16.0) * (here[i] * here[j])
                term = leonard * model
                lm_sum = term if lm_sum is None else lm_sum + term
                square = model * model
                if q < 3:
                    diag = square if diag is None else diag + square
                else:
                    off = square if off is None else off + square
            lm_term = lm_sum * (1.0 / 512.0)
            mm_term = (2.0 * diag + off) * (1.0 / 2048.0)
            lm_up, mm_up = averages_up(frame, ea, up[shifts[0], :], up[shifts[1], :], plane, cell)
            ratio = (0.2 / 1.5) * jnp.sqrt(jnp.sqrt(jnp.sqrt(lm_up * mm_up)))
            inverse = 1.0 / (1.0 + ratio)
            lm_new = jnp.maximum((ratio * lm_term + lm_up) * inverse, 0.0)
            mm_new = (ratio * mm_term + mm_up) * inverse
            smag = 0.5 * mags[pl.ds(frame.magnitude(plane, cell), 8), :]
            if frame.turned:
                where_at = pl.ds(skipped + plane, 8, stride=8)
            else:
                where_at = pl.ds(plane * CY + cell, 8)
            for out, value in zip(outs, (lm_new, mm_new, lm_new / mm_new * smag)):
                out[where_at, :] = value


def split(values):
    high = values.astype(jnp.bfloat16)
    return high, (values - high.astype(F32)).astype(jnp.bfloat16)


def dot_over(a, b, dims):
    (a_high, a_low), (b_high, b_low) = split(a), split(b)

    def dot(x, y):
        return lax.dot_general(x, y, (dims, ((), ())), preferred_element_type=F32)

    return dot(a_high, b_high) + dot(a_high, b_low) + dot(a_low, b_high)


def turbines(blocks, shift_x, shift_y, in_rows, first, span, out_rows, out_at, eu, total, keep):
    begin, stride, columns_out = out_at
    cell_x = lax.broadcasted_iota(jnp.int32, (24, 128), 0).astype(F32) - 5.0 - shift_x
    cell_y = lax.broadcasted_iota(jnp.int32, (span, 256), 0).astype(F32) + shift_y
    cell_z = lax.broadcasted_iota(jnp.int32, (ZSPAN, 256), 0).astype(F32) + float(ZLOW)
    weights_x = [weight(cell_x - block[6:7, :]) for block in blocks]
    planes = [None] * len(blocks)
    for row in in_rows:
        values = eu[pl.ds((row + 5) * PY + first, span), :]
        for t, weight_x in enumerate(weights_x):
            term = weight_x[row + 5 : row + 6, :] * values
            planes[t] = term if planes[t] is None else planes[t] + term
    patches = []
    for block, plane in zip(blocks, planes):
        pos_y = jnp.concatenate([block[0:1, :], block[1:2, :]], axis=1)
        pos_z = jnp.concatenate([block[2:3, :], block[3:4, :]], axis=1)
        strength = jnp.concatenate([block[4:5, :], block[5:6, :]], axis=1)
        strength = jnp.where(keep(pos_y), strength, 0.0)
        weight_y = weight(cell_y - pos_y)
        weight_z = weight(cell_z - pos_z)
        columns = dot_over(plane.T, weight_y, ((1,), (0,)))
        sampled = [
            jnp.sum(columns[c * ZSPAN : (c + 1) * ZSPAN, :] * weight_z, axis=0, keepdims=True)
            for c in range(3)
        ]
        speed = jnp.sqrt(sampled[0] * sampled[0] + sampled[1] * sampled[1] + sampled[2] * sampled[2])
        scale = -(strength * speed)
        spread = [weight_z * (scale * sampled[c]) for c in range(3)]
        spread = jnp.concatenate(spread + [jnp.zeros((8, 256), F32)], axis=0)
        rows_y = weight_y[8 : 8 + CY, :] if columns_out == CY else weight_y
        patches.append(dot_over(rows_y, spread, ((1,), (1,))))
    for row in out_rows:
        where_at = pl.ds(row * stride + begin, columns_out)
        value = total[where_at, :]
        for weight_x, patch in zip(weights_x, patches):
            value = value + weight_x[row + 5 : row + 6, :] * patch
        total[where_at, :] = value


def inside(pos_y):
    return (pos_y >= 2.0) & (pos_y <= float(CY - 3))


def unpack(values):
    lane = lax.broadcasted_iota(jnp.int32, values.shape, 1)
    held = (lane >= ZLOW) & (lane < ZLOW + ZSPAN)
    shifts = (ZLOW, NZ + ZLOW - ZSPAN, NZ + ZLOW - 2 * ZSPAN)
    return [jnp.where(held, pltpu.roll(values, shift % NZ, 1), 0.0) for shift in shifts]


def interior(
    vel, lm, mm, up, slab, points, xlow, xhigh, ulow, uhigh,
    lm_next, mm_next, visc, body, rims, total_rims, eu, tv, ta,
    ev, ea, xs, uh, mags, total, results, forces, sems,
):
    assemble(vel, lm, mm, slab, xlow, xhigh, ulow, uhigh, ev, ea, eu, tv, ta)
    closure_first(ROWS, ev, xs, mags, (1, 9, 17, 23))
    closure_hat(ROWS, xs, uh, (2, 10, 18, 22))
    field = CX * CY
    outs = [results.at[pl.ds(i * field, field), :] for i in range(3)]
    closure_last(ROWS, ea, up, xs, uh, mags, outs, (3, 11, 19, 21))
    copies = []

    def send(source, target):
        copies.append(pltpu.make_async_copy(source, target, sems.at[len(copies)]))
        copies[-1].start()

    for out, target in zip(outs, (lm_next, mm_next, visc)):
        send(out, target)
    total[...] = jnp.zeros((field, 128), F32)
    for source, base, shift_x, in_rows, out_rows in (
        (points, 0, 0.0, range(-2, 11), range(0, 8)),
        (xlow, 480, -8.0, range(-5, 3), range(0, 3)),
        (xhigh, 480, 8.0, range(6, 13), range(6, 8)),
    ):
        blocks = [source[pl.ds(base + t * 8, 8), :] for t in range(TURBINES)]
        turbines(blocks, shift_x, -8.0, in_rows, 0, PY, out_rows, (0, CY, CY), eu, total, inside)
    for row in range(CX):
        values = total[pl.ds(row * CY, CY), :]
        for c, out in enumerate(unpack(values)):
            forces[pl.ds((c * CX + row) * CY, CY), :] = out
        for side, col in ((0, 0), (1, CY - 8)):
            total_rims[pl.ds((side * CX + row) * 8, 8), :] = values[col : col + 8, :]
            for i in range(3):
                rims[pl.ds(((i * 2 + side) * CX + row) * 8, 8), :] = results[
                    pl.ds(i * field + row * CY + col, 8), :
                ]
    send(forces, body)
    for copy in copies:
        copy.wait()


def rim_hits(everyone):
    scalars = []
    for end in range(2):
        lines = []
        for near in (True, False):
            base = 0 if near else 72 + 72 * end

            def line(q, base=base):
                return jnp.concatenate(
                    [
                        everyone[pl.ds(base + q, 8, stride=8), :],
                        everyone[pl.ds(base + 64 + q, 1), :],
                    ],
                    axis=0,
                )

            late = near == (end == 1)
            hit = None
            for half in range(2):
                pos_y = line(half)
                found = (pos_y > float(CY - 3)) if late else (pos_y < 2.0)
                found = found & (line(4 + half) > 0.0)
                hit = found if hit is None else hit | found
            place = lax.broadcasted_iota(jnp.int32, (9, 128), 0)
            pos_x = line(6)
            left = (place >= 3) & (place < 6)
            hit = hit & (pos_x > jnp.where(left, 5.0, -1.0))
            hit = hit & (pos_x < jnp.where(place < 6, float(CX + 1), 2.0))
            lines.append(jnp.max(hit.astype(F32), axis=1, keepdims=True))
        place = lax.broadcasted_iota(jnp.int32, (9, 1), 0)
        bits = lax.shift_left(jnp.ones((9, 1), jnp.int32), place).astype(F32)
        scalars.append(jnp.sum(bits * (lines[0] + 512.0 * lines[1])).astype(jnp.int32))
    return scalars


def rim_batch(items, eu, total, everyone):
    cell_x = lax.broadcasted_iota(jnp.int32, (24, 128), 0).astype(F32) - 5.0
    cell_y = lax.broadcasted_iota(jnp.int32, (16, 256), 0).astype(F32)
    cell_z = lax.broadcasted_iota(jnp.int32, (ZSPAN, 256), 0).astype(F32) + float(ZLOW)
    ready = []
    for item in items:
        end = jnp.where((item >= 18) & (item < 36), 1, 0)
        number = item - 18 * end
        beyond = number >= 9
        place = jnp.where(beyond, number - 9, number)
        block_at = jnp.where(beyond, 9 + 9 * end, 0) + place
        block_at = jnp.where(item >= 36, 27, block_at)
        block = everyone[pl.ds(pl.multiple_of(block_at * 8, 8), 8), :]
        shift_x = jnp.where(place < 3, 0.0, jnp.where(place < 6, -8.0, 8.0))
        late = jnp.where(beyond, 1 - end, end) == 1
        shift_y = jnp.where(late, 24.0, -8.0)
        lowest = jnp.where(late, float(CY - 3), -1.0)
        highest = jnp.where(late, float(CY + 1), 2.0)
        weight_x = weight(cell_x - shift_x - block[6:7, :])
        terms = []
        first = pl.multiple_of(end * 32, 8)
        for row in range(18):
            terms.append(weight_x[row : row + 1, :] * eu[pl.ds(row * PY + first, 16), :])
        while len(terms) > 1:
            terms = [sum(terms[i + 1 : i + 2], terms[i]) for i in range(0, len(terms), 2)]
        pos_y = jnp.concatenate([block[0:1, :], block[1:2, :]], axis=1)
        pos_z = jnp.concatenate([block[2:3, :], block[3:4, :]], axis=1)
        strength = jnp.concatenate([block[4:5, :], block[5:6, :]], axis=1)
        strength = jnp.where((pos_y > lowest) & (pos_y < highest), strength, 0.0)
        ready.append((end, weight_x, terms[0], weight(cell_y + shift_y - pos_y), weight(cell_z - pos_z), strength))
    patches = []
    for end, weight_x, plane, weight_y, weight_z, strength in ready:
        columns = dot_over(plane.T, weight_y, ((1,), (0,)))
        sampled = [
            jnp.sum(columns[c * ZSPAN : (c + 1) * ZSPAN, :] * weight_z, axis=0, keepdims=True)
            for c in range(3)
        ]
        speed = jnp.sqrt(sampled[0] * sampled[0] + sampled[1] * sampled[1] + sampled[2] * sampled[2])
        scale = -(strength * speed)
        spread = [weight_z * (scale * sampled[c]) for c in range(3)]
        spread = jnp.concatenate(spread + [jnp.zeros((8, 256), F32)], axis=0)
        patches.append(dot_over(weight_y, spread, ((1,), (1,))))
    for patch, (end, weight_x, *_) in zip(patches, ready):
        for row in range(CX):
            where_at = pl.ds(pl.multiple_of((end * CX + row) * 16, 8), 16)
            total[where_at, :] += weight_x[row + 5 : row + 6, :] * patch


def edges(
    up, points, xlow, xhigh, ylow, yhigh, rims, total_rims, eu_in, tv_in, ta_in,
    lm_given, mm_given, visc_given, body_given,
    lm_next, mm_next, visc, body,
    tv, ta, eu, xs, uh, mags, total, everyone, results, forces, listed, sems,
):
    everyone[pl.ds(0, 24), :] = points[...]
    everyone[pl.ds(24, 24), :] = xlow[pl.ds(480, 24), :]
    everyone[pl.ds(48, 24), :] = xhigh[pl.ds(480, 24), :]
    everyone[pl.ds(72, 72), :] = ylow[pl.ds(YP, 72), :]
    everyone[pl.ds(144, 72), :] = yhigh[pl.ds(YP, 72), :]
    everyone[pl.ds(216, 8), :] = jnp.zeros((8, 128), F32)
    hits = rim_hits(everyone)
    found = jnp.int32(0)
    for item in range(36):
        listed[found] = jnp.int32(item)
        found = found + lax.rem(lax.shift_right_logical(hits[item // 18], item % 18), 2)
    for i in range(3):
        listed[found + i] = jnp.int32(36)
    tv[...] = tv_in[...]
    ta[...] = ta_in[...]
    eu[...] = eu_in[...]
    for side in range(2):
        for row in range(CX):
            total[pl.ds((side * CX + row) * 16 + 8 - 8 * side, 8), :] = total_rims[
                pl.ds((side * CX + row) * 8, 8), :
            ]
    complete(ylow, yhigh, tv, ta, eu)
    results[...] = rims[...]
    size_v, size_a, *sizes = SIDE.sizes()
    copies = []

    def send(source, target, col):
        target = target.at[..., pl.ds(col, 8), :]
        copies.append(pltpu.make_async_copy(source, target, sems.at[len(copies)]))
        copies[-1].start()

    for side, first, skipped in ((0, 0, 0), (1, CY - 3, 5)):
        velocity = tv.at[pl.ds(side * size_v, size_v), :]
        averages = ta.at[pl.ds(side * size_a, size_a), :]
        own = [ref.at[pl.ds(side * n, n), :] for ref, n in zip((xs, uh, mags), sizes)]
        closure_first(SIDE, velocity, own[0], own[2], (-2, 2))
        closure_hat(SIDE, own[0], own[1], (-1, 1))
        outs = [results.at[pl.ds((i * 2 + side) * 64, 64), :] for i in range(3)]
        closure_last(SIDE, averages, up, *own, outs, (0,), first, skipped)
    for side in range(2):
        for i, target in enumerate((lm_next, mm_next, visc)):
            part = results.at[pl.ds((i * 2 + side) * 64, 64), :]
            send(part.reshape(CX, 8, NZ), target, side * (CY - 8))

    def batch(i, carry):
        rim_batch([listed[3 * i + t] for t in range(3)], eu, total, everyone)
        return carry

    lax.fori_loop(0, lax.div(found + 2, 3), batch, 0)
    for side in range(2):
        for row in range(CX):
            values = total[pl.ds((side * CX + row) * 16 + 8 - 8 * side, 8), :]
            for c, out in enumerate(unpack(values)):
                forces[pl.ds(((side * 3 + c) * CX + row) * 8, 8), :] = out
        part = forces.at[pl.ds(side * 192, 192), :]
        send(part.reshape(3, CX, 8, NZ), body, side * (CY - 8))
    for copy in copies:
        copy.wait()


VMEM = pl.BlockSpec(memory_space=pltpu.VMEM)
HBM = pl.BlockSpec(memory_space=pltpu.HBM)


def rows(count):
    return jax.ShapeDtypeStruct((count, 128), F32)


def limit(mebibytes):
    return pltpu.CompilerParams(vmem_limit_bytes=mebibytes * 1024 * 1024)


def shards(velocity, lm_old, mm_old, upstream, point_pos, point_coef, tile_turbines):
    field = CX * CY
    up = upstream.reshape(2 * field, NZ)
    inputs = (
        velocity.reshape(3 * field, NZ),
        lm_old.reshape(field, NZ),
        mm_old.reshape(field, NZ),
        point_pos.reshape(3, 1, TURBINES * SLOTS),
        point_coef[0],
    )
    low, high, slab, points, vel, lm, mm = pl.pallas_call(
        pack_x,
        out_shape=[rows(n) for n in (XMSG, XMSG, field, 24, 3 * field, field, field)],
        in_specs=[HBM] * 5 + [pl.BlockSpec(memory_space=pl.ANY)],
        out_specs=[VMEM] * 7,
        scratch_shapes=[
            pltpu.VMEM((3, 1, TURBINES * SLOTS), F32),
            pltpu.VMEM((1, TURBINES * SLOTS), F32),
            pltpu.VMEM((1, 1), jnp.int32),
            pltpu.SemaphoreType.DMA((6,)),
        ],
        compiler_params=limit(8),
        name="pack_x",
    )(*(pltpu.with_memory_space_constraint(value, pltpu.HBM) for value in inputs), tile_turbines)
    xlow = shifted(high, "gx", 1)
    xhigh = shifted(low, "gx", -1)
    low, high, ulow, uhigh = pl.pallas_call(
        pack_y,
        out_shape=(rows(YMSG), rows(YMSG), rows(64), rows(64)),
        in_specs=[VMEM] * 7,
        out_specs=(VMEM,) * 4,
        compiler_params=limit(8),
        name="pack_y",
    )(vel, lm, mm, slab, points, xlow, xhigh)
    ylow = shifted(high, "gy", 1)
    yhigh = shifted(low, "gy", -1)
    size_v, size_a, *sizes = SIDE.sizes()
    handed = [3 * 2 * 64, 2 * 64, 18 * PY, 2 * size_v, 2 * size_a]
    final = [pltpu.HBM((n, NZ), F32) for n in (field, field, field, 3 * field)]
    first = pl.pallas_call(
        interior,
        out_shape=final + [rows(n) for n in handed],
        in_specs=[VMEM] * 10,
        out_specs=[HBM] * 4 + [VMEM] * 5,
        scratch_shapes=[
            pltpu.VMEM((n, 128), F32) for n in (*ROWS.sizes(), field, 3 * field, 3 * field)
        ]
        + [pltpu.SemaphoreType.DMA((4,))],
        compiler_params=limit(16),
        cost_estimate=pl.CostEstimate(flops=20_000_000, bytes_accessed=20_000_000, transcendentals=0),
        name="interior",
    )(vel, lm, mm, up, slab, points, xlow, xhigh, ulow, uhigh)
    shape = (CX, CY, NZ)
    shapes = [shape, shape, shape, (3, *shape)]
    given = [
        pltpu.with_memory_space_constraint(value.reshape(s), pltpu.HBM)
        for value, s in zip(first, shapes)
    ]
    eu, tv, ta = handed[2:]
    own = [tv, ta, eu, *(2 * n for n in sizes), 2 * CX * 16, 28 * 8, 3 * 2 * 64, 3 * 2 * 64]
    return pl.pallas_call(
        edges,
        out_shape=[pltpu.HBM(s, F32) for s in shapes],
        in_specs=[VMEM] * 11 + [HBM] * 4,
        out_specs=[HBM] * 4,
        input_output_aliases={11: 0, 12: 1, 13: 2, 14: 3},
        scratch_shapes=[pltpu.VMEM((n, 128), F32) for n in own]
        + [pltpu.SMEM((40,), jnp.int32), pltpu.SemaphoreType.DMA((8,))],
        compiler_params=limit(16),
        name="edges",
    )(up, points, xlow, xhigh, ylow, yhigh, *first[4:], *given)


def solution(mesh):
    return jax.shard_map(
        shards,
        mesh=mesh,
        in_specs=(
            P(None, "gx", "gy", None),
            P("gx", "gy", None),
            P("gx", "gy", None),
            P(None, "gx", "gy", None),
            P("gx", "gy", None, None),
            P("gx", "gy", None),
            P("gx", "gy"),
        ),
        out_specs=(
            P("gx", "gy", None),
            P("gx", "gy", None),
            P("gx", "gy", None),
            P(None, "gx", "gy", None),
        ),
        check_vma=False,
    )
```

```python
import math

import jax
import jax.numpy as jnp
from jax import lax
from jax.experimental import pallas as pl
from jax.experimental.pallas import tpu as pltpu
from jax.sharding import PartitionSpec as P

F32 = jnp.float32
CX, CY, NZ = 8, 32, 128
TURBINES, SLOTS = 3, 192
ZLOW, ZSPAN = 46, 40
XMSG = 496
YMSG = 272
YA, YU, YN, YP = 72, 156, 210, 224
EY = 40
PY = 48


def shifted(block, axis, distance):
    count = lax.axis_size(axis)
    return lax.ppermute(block, axis, [(i, (i + distance) % count) for i in range(count)])


def weight(offset):
    scaled = offset * (1.0 / 1.5)
    return jnp.maximum(jnp.exp(-(scaled * scaled)) - math.exp(-4.0), 0.0)


def packed(parts):
    lane = lax.broadcasted_iota(jnp.int32, parts[0].shape, 1)
    first = pltpu.roll(parts[0], NZ - ZLOW, 1)
    second = pltpu.roll(parts[1], NZ + ZSPAN - ZLOW, 1)
    third = pltpu.roll(parts[2], 2 * ZSPAN - ZLOW, 1)
    rest = jnp.where(lane < 3 * ZSPAN, third, 0.0)
    return jnp.where(lane < ZSPAN, first, jnp.where(lane < 2 * ZSPAN, second, rest))


def pack_x(
    vel_in, lm_in, mm_in, pos_in, coef_in, count_in,
    low, high, slab, points, vel, lm, mm, pos, coef, count, sems,
):
    pairs = (
        (vel_in, vel), (pos_in, pos), (coef_in, coef), (count_in, count), (lm_in, lm), (mm_in, mm),
    )
    copies = [pltpu.make_async_copy(x, y, sems.at[i]) for i, (x, y) in enumerate(pairs)]
    for copy in copies:
        copy.start()
    for copy in copies[1:4]:
        copy.wait()
    lane = lax.broadcasted_iota(jnp.int32, (1, 128), 1)
    turbine_count = jnp.broadcast_to(count[...], (1, 128))
    early = lane < 64
    for t in range(TURBINES):
        at = t * SLOTS
        (pos_x, _), (y_first, y_rest), (z_first, z_rest), (s_first, s_rest) = [
            (values[:, at : at + 128], values[:, at + 64 : at + 192])
            for values in (pos[0], pos[1], pos[2], coef[...])
        ]
        live = turbine_count > t
        lines = [
            y_first,
            z_first,
            jnp.where(live, s_first, 0.0),
            jnp.where(early, pltpu.roll(z_rest, 64, 1), y_rest),
            jnp.where(early, pos_x, jnp.where(live, s_rest, 0.0)),
        ]
        block = jnp.concatenate(lines, axis=0)
        for out, base in ((low, 480), (high, 480), (points, 0)):
            out[pl.ds(base + 5 * t, 5), :] = block
    for out, base in ((low, 495), (high, 495), (points, 15)):
        out[pl.ds(base, 1), :] = jnp.zeros((1, 128), F32)
    copies[0].wait()
    for row in range(CX):
        parts = [vel[pl.ds((c * CX + row) * CY, CY), :] for c in range(3)]
        value = packed(parts)
        slab[pl.ds(row * CY, CY), :] = value
        if 2 <= row < 5:
            low[pl.ds(384 + (row - 2) * CY, CY), :] = value
        if 3 <= row < 6:
            high[pl.ds(384 + (row - 3) * CY, CY), :] = value
        for out, first in ((low, 0), (high, CX - 2)):
            if first <= row < first + 2:
                for c in range(3):
                    out[pl.ds(c * 64 + (row - first) * CY, CY), :] = parts[c]
    copies[4].wait()
    copies[5].wait()
    for out, first in ((low, 0), (high, CX - 3)):
        for f, own in enumerate((lm, mm)):
            out[pl.ds(192 + f * 96, 96), :] = own[pl.ds(first * CY, 96), :]


def pack_y(vel, lm, mm, slab, points, xlow, xhigh, low, high, ulow, uhigh):
    for out, message in ((ulow, xlow), (uhigh, xhigh)):
        for i in range(2):
            parts = [message[pl.ds(c * 64 + i * CY, CY), :] for c in range(3)]
            out[pl.ds(i * CY, CY), :] = packed(parts)
    for out, col_v, col_a, col_u in ((low, 0, 0, 0), (high, CY - 2, CY - 3, CY - 5)):
        for c in range(3):
            for j in range(2):
                base, col = (c * 2 + j) * 12, col_v + j
                out[pl.ds(base, 2), :] = xlow[pl.ds(c * 64 + col, 2, stride=CY), :]
                out[pl.ds(base + 2, 8), :] = vel[pl.ds(c * 256 + col, 8, stride=CY), :]
                out[pl.ds(base + 10, 2), :] = xhigh[pl.ds(c * 64 + col, 2, stride=CY), :]
        for f, own in enumerate((lm, mm)):
            for j in range(3):
                base, col = YA + (f * 3 + j) * 14, col_a + j
                out[pl.ds(base, 3), :] = xlow[pl.ds(192 + f * 96 + col, 3, stride=CY), :]
                out[pl.ds(base + 3, 8), :] = own[pl.ds(col, 8, stride=CY), :]
                out[pl.ds(base + 11, 3), :] = xhigh[pl.ds(192 + f * 96 + col, 3, stride=CY), :]
        far, near = (col_u, col_u + 3) if col_v else (col_u + 2, col_u)
        for j in range(3):
            base, col = YU + j * 18, far + j
            out[pl.ds(base, 3), :] = xlow[pl.ds(384 + col, 3, stride=CY), :]
            out[pl.ds(base + 3, 2), :] = ulow[pl.ds(col, 2, stride=CY), :]
            out[pl.ds(base + 5, 8), :] = slab[pl.ds(col, 8, stride=CY), :]
            out[pl.ds(base + 13, 2), :] = uhigh[pl.ds(col, 2, stride=CY), :]
            out[pl.ds(base + 15, 3), :] = xhigh[pl.ds(384 + col, 3, stride=CY), :]
        for j in range(2):
            base, col = YN + j * 6, near + j
            out[pl.ds(base, 3), :] = xlow[pl.ds(384 + col, 3, stride=CY), :]
            out[pl.ds(base + 3, 3), :] = xhigh[pl.ds(384 + col, 3, stride=CY), :]
        out[pl.ds(YN + 12, 2), :] = jnp.zeros((2, 128), F32)
        for k, source in enumerate((points, xlow, xhigh)):
            first = 0 if k == 0 else 480
            out[pl.ds(YP + 15 * k, 15), :] = source[pl.ds(first, 15), :]
        out[pl.ds(YP + 45, 3), :] = jnp.zeros((3, 128), F32)


def expand(source, base, out, out_base, count):
    early = lax.broadcasted_iota(jnp.int32, (1, 128), 1) < 64
    for t in range(count):
        block = source[pl.ds(base + 5 * t, 5), :]
        turned = pltpu.roll(block[3:5, :], 64, 1)
        lines = [
            block[0:1, :],
            block[3:4, :],
            block[1:2, :],
            turned[0:1, :],
            block[2:3, :],
            jnp.where(early, 0.0, block[4:5, :]),
            jnp.where(early, block[4:5, :], turned[1:2, :]),
            jnp.where(early, block[4:5, :], turned[1:2, :]),
        ]
        out[pl.ds(out_base + 8 * t, 8), :] = jnp.concatenate(lines, axis=0)


class Frame:
    def __init__(self, planes, width, turned):
        self.planes, self.width, self.turned = planes, width, turned

    def velocity(self, c, plane, cell):
        return (c * (self.planes + 4) + plane + 2) * self.width + cell + 4

    def average(self, f, plane, cell):
        return (f * (self.planes + 6) + plane + 3) * self.width + cell + 4

    def summed(self, q, plane, cell):
        return (q * (self.planes + 2) + plane + 1) * self.width + cell + 4

    def magnitude(self, plane, cell):
        return plane * self.width + cell + 4

    def sizes(self):
        n, w = self.planes, self.width
        return 3 * (n + 4) * w, 2 * (n + 6) * w, 15 * (n + 2) * w, 3 * (n + 2) * w, n * w


ROWS = Frame(CX, EY, False)
SIDE = Frame(3, 16, True)


def assemble(vel, lm, mm, slab, xlow, xhigh, ulow, uhigh, ev, ea, eu, ends):
    for c in range(3):
        for row in range(CX):
            ev[pl.ds(ROWS.velocity(c, row, 0), CY), :] = vel[pl.ds((c * CX + row) * CY, CY), :]
        for i in range(2):
            ev[pl.ds(ROWS.velocity(c, i - 2, 0), CY), :] = xlow[pl.ds(c * 64 + i * CY, CY), :]
            ev[pl.ds(ROWS.velocity(c, i + 8, 0), CY), :] = xhigh[pl.ds(c * 64 + i * CY, CY), :]
    for f, own in enumerate((lm, mm)):
        for row in range(CX):
            ea[pl.ds(ROWS.average(f, row, 0), CY), :] = own[pl.ds(row * CY, CY), :]
        for i in range(3):
            source = 192 + f * 96 + i * CY
            ea[pl.ds(ROWS.average(f, i - 3, 0), CY), :] = xlow[pl.ds(source, CY), :]
            ea[pl.ds(ROWS.average(f, i + 8, 0), CY), :] = xhigh[pl.ds(source, CY), :]
    zero = jnp.zeros((8, 128), F32)
    for row in range(18):
        eu[pl.ds(row * PY, 8), :] = zero
        eu[pl.ds(row * PY + 40, 8), :] = zero
    for row in range(CX):
        eu[pl.ds((row + 5) * PY + 8, CY), :] = slab[pl.ds(row * CY, CY), :]
    for i in range(3):
        eu[pl.ds(i * PY + 8, CY), :] = xlow[pl.ds(384 + i * CY, CY), :]
        eu[pl.ds((i + 15) * PY + 8, CY), :] = xhigh[pl.ds(384 + i * CY, CY), :]
    for i in range(2):
        eu[pl.ds((i + 3) * PY + 8, CY), :] = ulow[pl.ds(i * CY, CY), :]
        eu[pl.ds((i + 13) * PY + 8, CY), :] = uhigh[pl.ds(i * CY, CY), :]
    for end, (packed_end, tv, ta) in enumerate(ends):
        first = end * (CY - 3)
        for c in range(3):
            for plane in range(-2, 3) if end else range(5):
                source, target = ROWS.velocity(c, 0, first + plane), SIDE.velocity(c, plane, 0)
                for start, count in ((-2, 8), (6, 4)):
                    tv[pl.ds(target + start, count), :] = ev[
                        pl.ds(source + start * EY, count, stride=EY), :
                    ]
        for f in range(2):
            for plane in range(-3, 3) if end else range(6):
                source, target = ROWS.average(f, 0, first + plane), SIDE.average(f, plane, 0)
                for start, count in ((-3, 8), (3, 8)):
                    ta[pl.ds(target + start, count), :] = ea[
                        pl.ds(source + start * EY, count, stride=EY), :
                    ]
        for row in range(18):
            packed_end[pl.ds(row * 16, 16), :] = eu[pl.ds(row * PY + end * 32, 16), :]


def complete(end, message, eu, tv, ta):
    plane_v, plane_a, first = (3, 3, 8) if end else (-2, -3, 3)
    for c in range(3):
        for j in range(2):
            target = SIDE.velocity(c, plane_v + j, -2)
            tv[pl.ds(target, 12), :] = message[pl.ds((c * 2 + j) * 12, 12), :]
    for f in range(2):
        for j in range(3):
            target = SIDE.average(f, plane_a + j, -3)
            ta[pl.ds(target, 14), :] = message[pl.ds(YA + (f * 3 + j) * 14, 14), :]
    far, near = (first + 2, first) if end else (first, first + 3)
    for j in range(3):
        for start, count in ((0, 8), (8, 8), (16, 2)):
            eu[pl.ds(start * 16 + far + j, count, stride=16), :] = message[
                pl.ds(YU + j * 18 + start, count), :
            ]
    for j in range(2):
        for start, source in ((0, 0), (15, 3)):
            eu[pl.ds(start * 16 + near + j, 3, stride=16), :] = message[
                pl.ds(YN + j * 6 + source, 3), :
            ]
        for start, count in ((0, 8), (8, 4)):
            parts = [message[pl.ds((c * 2 + j) * 12 + start, count), :] for c in range(3)]
            eu[pl.ds((start + 3) * 16 + near + j, count, stride=16), :] = packed(parts)


PAIRS = ((0, 0), (1, 1), (2, 2), (0, 1), (0, 2), (1, 2))


def slope_z(values):
    lane = lax.broadcasted_iota(jnp.int32, values.shape, 1)
    above = jnp.where(lane == NZ - 1, values, pltpu.roll(values, NZ - 1, 1))
    below = jnp.where(lane == 0, values, pltpu.roll(values, 1, 1))
    return above - below


def tensor_of(slopes):
    parts = [slopes[0][0], slopes[1][1], slopes[2][2]]
    parts += [slopes[j][i] + slopes[i][j] for i, j in PAIRS[3:]]
    diag = parts[0] * parts[0] + parts[1] * parts[1] + parts[2] * parts[2]
    off = parts[3] * parts[3] + parts[4] * parts[4] + parts[5] * parts[5]
    return parts, jnp.sqrt(2.0 * diag + off)


def closure_first(frame, ev, xs, mags, starts):
    def at(c, plane, cell):
        return ev[pl.ds(frame.velocity(c, plane, cell), 8), :]

    def put(q, plane, cell, value):
        xs[pl.ds(frame.summed(q, plane, cell), 8), :] = value

    for cell in starts:
        before = [at(c, -2, cell) for c in range(3)]
        here = [at(c, -1, cell) for c in range(3)]
        history = []
        for plane in range(-1, frame.planes + 1):
            after = [at(c, plane + 1, cell) for c in range(3)]
            slopes = [
                [after[c] - before[c] for c in range(3)],
                [at(c, plane, cell + 1) - at(c, plane, cell - 1) for c in range(3)],
            ]
            if frame.turned:
                slopes.reverse()
            slopes.append([slope_z(here[c]) for c in range(3)])
            parts, mag = tensor_of(slopes)
            now = [mag * part for part in parts] + [here[i] * here[j] for i, j in PAIRS]
            if 0 <= plane < frame.planes:
                mags[pl.ds(frame.magnitude(plane, cell), 8), :] = mag
            for c in range(3):
                put(12 + c, plane, cell, before[c] + (here[c] + here[c]) + after[c])
            history.append(now)
            if len(history) == 3:
                for q in range(12):
                    value = history[0][q] + (history[1][q] + history[1][q]) + history[2][q]
                    put(q, plane - 1, cell, value)
                history.pop(0)
            before, here = here, after


def closure_hat(frame, xs, uh, starts):
    for c in range(3):
        for plane in range(-1, frame.planes + 1):
            for cell in starts:
                base = frame.summed(12 + c, plane, cell)
                mid = xs[pl.ds(base, 8), :]
                value = xs[pl.ds(base - 1, 8), :] + (mid + mid) + xs[pl.ds(base + 1, 8), :]
                uh[pl.ds(frame.summed(c, plane, cell), 8), :] = value


def take_rows(values, index):
    return jnp.take_along_axis(values, index, axis=0)


def averages_up(frame, ea, shift_plane, shift_cell, plane, cell):
    sub = lax.broadcasted_iota(jnp.int32, (8, 128), 0)
    index = sub - shift_cell + 3
    early = index < 8
    first = jnp.minimum(index, 7)
    second = jnp.maximum(index - 6, 0)
    result = [None, None]
    for shift in range(-3, 4):
        chosen = shift_plane == shift
        for f in range(2):
            base = frame.average(f, plane - shift, cell)
            value = jnp.where(
                early,
                take_rows(ea[pl.ds(base - 3, 8), :], first),
                take_rows(ea[pl.ds(base + 3, 8), :], second),
            )
            result[f] = value if result[f] is None else jnp.where(chosen, value, result[f])
    return result


def closure_last(frame, ea, up, xs, uh, mags, outs, starts, first=0, skipped=0):
    def summed(q, plane, cell):
        base = frame.summed(q, plane, cell)
        mid = xs[pl.ds(base, 8), :]
        return xs[pl.ds(base - 1, 8), :] + (mid + mid) + xs[pl.ds(base + 1, 8), :]

    def hat(c, plane, cell):
        return uh[pl.ds(frame.summed(c, plane, cell), 8), :]

    for plane in range(frame.planes):
        for cell in starts:
            here = [hat(c, plane, cell) for c in range(3)]
            slopes = [
                [hat(c, plane + 1, cell) - hat(c, plane - 1, cell) for c in range(3)],
                [hat(c, plane, cell + 1) - hat(c, plane, cell - 1) for c in range(3)],
            ]
            shifts = [
                pl.ds(d * CX * CY + plane * CY + cell, 8)
                if not frame.turned
                else pl.ds(d * CX * CY + cell * CY + first + plane, 8, stride=CY)
                for d in range(2)
            ]
            if frame.turned:
                slopes.reverse()
                shifts.reverse()
            slopes.append([slope_z(here[c]) for c in range(3)])
            parts, mag = tensor_of(slopes)
            mag = 0.25 * mag
            lm_sum = diag = off = None
            for q, (i, j) in enumerate(PAIRS):
                model = summed(q, plane, cell) - mag * parts[q]
                leonard = summed(6 + q, plane, cell) - (1.0 / 16.0) * (here[i] * here[j])
                term = leonard * model
                lm_sum = term if lm_sum is None else lm_sum + term
                square = model * model
                if q < 3:
                    diag = square if diag is None else diag + square
                else:
                    off = square if off is None else off + square
            lm_term = lm_sum * (1.0 / 512.0)
            mm_term = (2.0 * diag + off) * (1.0 / 2048.0)
            lm_up, mm_up = averages_up(frame, ea, up[shifts[0], :], up[shifts[1], :], plane, cell)
            ratio = (0.2 / 1.5) * jnp.sqrt(jnp.sqrt(jnp.sqrt(lm_up * mm_up)))
            inverse = 1.0 / (1.0 + ratio)
            lm_new = jnp.maximum((ratio * lm_term + lm_up) * inverse, 0.0)
            mm_new = (ratio * mm_term + mm_up) * inverse
            smag = 0.5 * mags[pl.ds(frame.magnitude(plane, cell), 8), :]
            if frame.turned:
                where_at = pl.ds(skipped + plane, 8, stride=8)
            else:
                where_at = pl.ds(plane * CY + cell, 8)
            for out, value in zip(outs, (lm_new, mm_new, lm_new / mm_new * smag)):
                out[where_at, :] = value


def split(values):
    high = values.astype(jnp.bfloat16)
    return high, (values - high.astype(F32)).astype(jnp.bfloat16)


def dot_over(a, b, dims):
    (a_high, a_low), (b_high, b_low) = split(a), split(b)

    def dot(x, y):
        return lax.dot_general(x, y, (dims, ((), ())), preferred_element_type=F32)

    return dot(a_high, b_high) + dot(a_high, b_low) + dot(a_low, b_high)


def turbines(blocks, shift_x, shift_y, in_rows, first, span, out_rows, out_at, eu, total, keep):
    begin, stride, columns_out = out_at
    cell_x = lax.broadcasted_iota(jnp.int32, (24, 128), 0).astype(F32) - 5.0 - shift_x
    cell_y = lax.broadcasted_iota(jnp.int32, (span, 256), 0).astype(F32) + shift_y
    cell_z = lax.broadcasted_iota(jnp.int32, (ZSPAN, 256), 0).astype(F32) + float(ZLOW)
    weights_x = [weight(cell_x - block[6:7, :]) for block in blocks]
    planes = [None] * len(blocks)
    for row in in_rows:
        values = eu[pl.ds((row + 5) * PY + first, span), :]
        for t, weight_x in enumerate(weights_x):
            term = weight_x[row + 5 : row + 6, :] * values
            planes[t] = term if planes[t] is None else planes[t] + term
    patches = []
    for block, plane in zip(blocks, planes):
        pos_y = jnp.concatenate([block[0:1, :], block[1:2, :]], axis=1)
        pos_z = jnp.concatenate([block[2:3, :], block[3:4, :]], axis=1)
        strength = jnp.concatenate([block[4:5, :], block[5:6, :]], axis=1)
        strength = jnp.where(keep(pos_y), strength, 0.0)
        weight_y = weight(cell_y - pos_y)
        weight_z = weight(cell_z - pos_z)
        columns = dot_over(plane.T, weight_y, ((1,), (0,)))
        sampled = [
            jnp.sum(columns[c * ZSPAN : (c + 1) * ZSPAN, :] * weight_z, axis=0, keepdims=True)
            for c in range(3)
        ]
        speed = jnp.sqrt(sampled[0] * sampled[0] + sampled[1] * sampled[1] + sampled[2] * sampled[2])
        scale = -(strength * speed)
        spread = [weight_z * (scale * sampled[c]) for c in range(3)]
        spread = jnp.concatenate(spread + [jnp.zeros((8, 256), F32)], axis=0)
        rows_y = weight_y[8 : 8 + CY, :] if columns_out == CY else weight_y
        patches.append(dot_over(rows_y, spread, ((1,), (1,))))
    for row in out_rows:
        where_at = pl.ds(row * stride + begin, columns_out)
        value = total[where_at, :]
        for weight_x, patch in zip(weights_x, patches):
            value = value + weight_x[row + 5 : row + 6, :] * patch
        total[where_at, :] = value


def inside(pos_y):
    return (pos_y >= 2.0) & (pos_y <= float(CY - 3))


def unpack(values):
    lane = lax.broadcasted_iota(jnp.int32, values.shape, 1)
    held = (lane >= ZLOW) & (lane < ZLOW + ZSPAN)
    shifts = (ZLOW, NZ + ZLOW - ZSPAN, NZ + ZLOW - 2 * ZSPAN)
    return [jnp.where(held, pltpu.roll(values, shift % NZ, 1), 0.0) for shift in shifts]


def interior(
    vel, lm, mm, up, slab, points, xlow, xhigh, ulow, uhigh,
    results, forces, expanded, *refs,
):
    ends = refs[:5], refs[5:10]
    ev, ea, xs, uh, mags, total, eu = refs[10:]
    assemble(vel, lm, mm, slab, xlow, xhigh, ulow, uhigh, ev, ea, eu, [end[2:] for end in ends])
    closure_first(ROWS, ev, xs, mags, (1, 9, 17, 23))
    closure_hat(ROWS, xs, uh, (2, 10, 18, 22))
    field = CX * CY
    outs = [results.at[pl.ds(i * field, field), :] for i in range(3)]
    closure_last(ROWS, ea, up, xs, uh, mags, outs, (3, 11, 19, 21))
    total[...] = jnp.zeros((field, 128), F32)
    for k, source in enumerate((points, xlow, xhigh)):
        expand(source, 480 if k else 0, expanded, 24 * k, TURBINES)
    for base, shift_x, in_rows, out_rows in (
        (0, 0.0, range(-2, 11), range(0, 8)),
        (24, -8.0, range(-5, 3), range(0, 3)),
        (48, 8.0, range(6, 13), range(6, 8)),
    ):
        blocks = [expanded[pl.ds(base + t * 8, 8), :] for t in range(TURBINES)]
        turbines(blocks, shift_x, -8.0, in_rows, 0, PY, out_rows, (0, CY, CY), eu, total, inside)
    for row in range(CX):
        values = total[pl.ds(row * CY, CY), :]
        for c, out in enumerate(unpack(values)):
            forces[pl.ds((c * CX + row) * CY, CY), :] = out
        for end, (rim, total_rim, *_) in enumerate(ends):
            col = end * (CY - 8)
            total_rim[pl.ds(row * 16 + 8 - 8 * end, 8), :] = values[col : col + 8, :]
            for i in range(3):
                rim[pl.ds((i * CX + row) * 8, 8), :] = results[
                    pl.ds(i * field + row * CY + col, 8), :
                ]


def rim_hits(end, everyone):
    lines = []
    place = lax.broadcasted_iota(jnp.int32, (9, 128), 0)
    left = (place >= 3) & (place < 6)
    least, most = jnp.where(left, 5.0, -1.0), jnp.where(place < 6, float(CX + 1), 2.0)
    for beyond in range(2):

        def line(q, base=72 * beyond):
            parts = everyone[pl.ds(base + q, 8, stride=8), :], everyone[pl.ds(base + 64 + q, 1), :]
            return jnp.concatenate(parts, axis=0)

        hit = None
        for half in range(2):
            pos_y = line(half)
            found = (pos_y > float(CY - 3)) if end != beyond else (pos_y < 2.0)
            found = found & (line(4 + half) > 0.0)
            hit = found if hit is None else hit | found
        pos_x = line(6)
        hit = hit & (pos_x > least) & (pos_x < most)
        lines.append(jnp.max(hit.astype(F32), axis=1, keepdims=True))
    bits = lax.shift_left(
        jnp.ones((9, 1), jnp.int32), lax.broadcasted_iota(jnp.int32, (9, 1), 0)
    ).astype(F32)
    return jnp.sum(bits * (lines[0] + 512.0 * lines[1])).astype(jnp.int32)


def stacked_product(a, b, dims, axes):
    (a_high, a_low), (b_high, b_low) = split(a), split(b)
    a_terms = jnp.concatenate([a_high, a_high, a_low], axis=axes[0])
    b_terms = jnp.concatenate([b_high, b_low, b_high], axis=axes[1])
    return lax.dot_general(a_terms, b_terms, (dims, ((), ())), preferred_element_type=F32)


def rim_batch(end, items, eu, total, everyone):
    cell_x = lax.broadcasted_iota(jnp.int32, (24, 128), 0).astype(F32) - 5.0
    cell_y = lax.broadcasted_iota(jnp.int32, (16, 256), 0).astype(F32)
    cell_z = lax.broadcasted_iota(jnp.int32, (ZSPAN, 256), 0).astype(F32) + float(ZLOW)
    ready = []
    for item in items:
        beyond = item >= 9
        place = jnp.where(beyond, item - 9, item)
        block = everyone[pl.ds(pl.multiple_of(item * 8, 8), 8), :]
        shift_x = jnp.where(place < 3, 0.0, jnp.where(place < 6, -8.0, 8.0))
        late = jnp.logical_not(beyond) if end else beyond
        shift_y = jnp.where(late, 24.0, -8.0)
        lowest = jnp.where(late, float(CY - 3), -1.0)
        highest = jnp.where(late, float(CY + 1), 2.0)
        weight_x = weight(cell_x - shift_x - block[6:7, :])
        terms = [weight_x[row : row + 1, :] * eu[pl.ds(row * 16, 16), :] for row in range(18)]
        while len(terms) > 1:
            terms = [sum(terms[i + 1 : i + 2], terms[i]) for i in range(0, len(terms), 2)]
        pos_y = jnp.concatenate([block[0:1, :], block[1:2, :]], axis=1)
        pos_z = jnp.concatenate([block[2:3, :], block[3:4, :]], axis=1)
        strength = jnp.concatenate([block[4:5, :], block[5:6, :]], axis=1)
        strength = jnp.where((pos_y > lowest) & (pos_y < highest), strength, 0.0)
        weights = weight(cell_y + shift_y - pos_y), weight(cell_z - pos_z)
        ready.append((weight_x, terms[0], *weights, strength))
    patches = []
    for _, plane, weight_y, weight_z, strength in ready:
        columns = stacked_product(plane.T, weight_y, ((1,), (0,)), (1, 0))
        sampled = [
            jnp.sum(columns[c * ZSPAN : (c + 1) * ZSPAN, :] * weight_z, axis=0, keepdims=True)
            for c in range(3)
        ]
        speed = jnp.sqrt(sampled[0] * sampled[0] + sampled[1] * sampled[1] + sampled[2] * sampled[2])
        scale = -(strength * speed)
        spread = [weight_z * (scale * sampled[c]) for c in range(3)]
        spread = jnp.concatenate(spread + [jnp.zeros((8, 256), F32)], axis=0)
        patches.append(stacked_product(weight_y, spread, ((1,), (1,)), (1, 1)))
    for row in range(CX):
        value = total[pl.ds(row * 16, 16), :]
        for patch, (weight_x, *_) in zip(patches, ready):
            value = value + weight_x[row + 5 : row + 6, :] * patch
        total[pl.ds(row * 16, 16), :] = value


def finish(end, inputs, scratch, results, forces, closed, forced):
    up, expanded, message, rim_in, total_in, eu_in, tv_in, ta_in = inputs
    tv, ta, eu, xs, uh, mags, total, everyone, listed = scratch
    everyone[pl.ds(0, 72), :] = expanded[...]
    expand(message, YP, everyone, 72, 3 * TURBINES)
    everyone[pl.ds(144, 8), :] = jnp.zeros((8, 128), F32)
    hits = rim_hits(end, everyone)
    found = jnp.int32(0)
    for item in range(18):
        listed[found] = jnp.int32(item)
        found = found + lax.rem(lax.shift_right_logical(hits, item), 2)
    for i in range(3):
        listed[found + i] = jnp.int32(18)
    tv[...] = tv_in[...]
    ta[...] = ta_in[...]
    eu[...] = eu_in[...]
    total[...] = total_in[...]
    results[...] = rim_in[...]
    complete(end, message, eu, tv, ta)
    closure_first(SIDE, tv, xs, mags, (-2, 2))
    closure_hat(SIDE, xs, uh, (-1, 1))
    outs = [results.at[pl.ds(i * 64, 64), :] for i in range(3)]
    first, skipped = (CY - 3, 5) if end else (0, 0)
    closure_last(SIDE, ta, up, xs, uh, mags, outs, (0,), first, skipped)
    closed()

    def batch(i, carry):
        rim_batch(end, [listed[3 * i + t] for t in range(3)], eu, total, everyone)
        return carry

    def write():
        for row in range(CX):
            values = total[pl.ds(row * 16 + 8 - 8 * end, 8), :]
            for c, out in enumerate(unpack(values)):
                forces[pl.ds((c * CX + row) * 8, 8), :] = out

    if end == 0:
        lax.fori_loop(0, lax.div(found + 2, 3), batch, 0)
        write()
        return

    @pl.when(found > 0)
    def _():
        lax.fori_loop(0, lax.div(found + 2, 3), batch, 0)
        write()
        forced()


def edge_low(*refs):
    inner_results, inner_forces, results, forces = refs[8:12]
    *scratch, sems = refs[16:]
    field = CX * CY
    sources = [inner_results.at[pl.ds(i * field, field), :] for i in range(3)] + [inner_forces]
    copies = [
        pltpu.make_async_copy(source.reshape(*target.shape), target, sems.at[i])
        for i, (source, target) in enumerate(zip(sources, refs[12:16]))
    ]
    for copy in copies:
        copy.start()
    finish(0, refs[:8], scratch, results, forces, lambda: None, None)
    for copy in copies:
        copy.wait()


def edge_high(*refs):
    inputs, (low_results, low_forces), targets = refs[:8], refs[8:10], refs[14:18]
    results, forces, sems = refs[27:]
    copies = []

    def sent(source, target, i, end):
        columns = pl.ds(end * (CY - 8), 8)
        source = source.reshape(*target.shape[:-2], 8, NZ)
        return pltpu.make_async_copy(source, target.at[..., columns, :], sems.at[i])

    def fields(values, end):
        for i, target in enumerate(targets[:3]):
            copies.append(sent(values.at[pl.ds(i * 64, 64), :], target, len(copies), end))
            copies[-1].start()

    def forced():
        copy = sent(forces, targets[3], 7, 1)
        copy.start()
        copy.wait()

    fields(low_results, 0)
    copies.append(sent(low_forces, targets[3], len(copies), 0))
    copies[-1].start()
    finish(1, inputs, refs[18:27], results, forces, lambda: fields(results, 1), forced)
    for copy in copies:
        copy.wait()


VMEM = pl.BlockSpec(memory_space=pltpu.VMEM)
HBM = pl.BlockSpec(memory_space=pltpu.HBM)


def rows(count):
    return jax.ShapeDtypeStruct((count, 128), F32)


def limit(mebibytes):
    return pltpu.CompilerParams(vmem_limit_bytes=mebibytes * 1024 * 1024)


def shards(velocity, lm_old, mm_old, upstream, point_pos, point_coef, tile_turbines):
    field = CX * CY
    up = upstream.reshape(2 * field, NZ)
    inputs = (
        velocity.reshape(3 * field, NZ),
        lm_old.reshape(field, NZ),
        mm_old.reshape(field, NZ),
        point_pos.reshape(3, 1, TURBINES * SLOTS),
        point_coef[0],
    )
    low, high, slab, points, vel, lm, mm = pl.pallas_call(
        pack_x,
        out_shape=[rows(n) for n in (XMSG, XMSG, field, 16, 3 * field, field, field)],
        in_specs=[HBM] * 5 + [pl.BlockSpec(memory_space=pl.ANY)],
        out_specs=[VMEM] * 7,
        scratch_shapes=[
            pltpu.VMEM((3, 1, TURBINES * SLOTS), F32),
            pltpu.VMEM((1, TURBINES * SLOTS), F32),
            pltpu.VMEM((1, 1), jnp.int32),
            pltpu.SemaphoreType.DMA((6,)),
        ],
        compiler_params=limit(8),
        name="pack_x",
    )(*(pltpu.with_memory_space_constraint(value, pltpu.HBM) for value in inputs), tile_turbines)
    xlow = shifted(high, "gx", 1)
    xhigh = shifted(low, "gx", -1)
    low, high, ulow, uhigh = pl.pallas_call(
        pack_y,
        out_shape=(rows(YMSG), rows(YMSG), rows(64), rows(64)),
        in_specs=[VMEM] * 7,
        out_specs=(VMEM,) * 4,
        compiler_params=limit(8),
        name="pack_y",
    )(vel, lm, mm, slab, points, xlow, xhigh)
    ylow = shifted(high, "gy", 1)
    yhigh = shifted(low, "gy", -1)
    size_v, size_a, *sizes = SIDE.sizes()
    handed = [3 * 64, CX * 16, 18 * 16, size_v, size_a]
    work = [*ROWS.sizes(), field, 18 * PY]
    first = pl.pallas_call(
        interior,
        out_shape=[rows(n) for n in (3 * field, 3 * field, 9 * 8, *handed, *handed)],
        in_specs=[VMEM] * 10,
        out_specs=[VMEM] * 13,
        scratch_shapes=[pltpu.VMEM((n, 128), F32) for n in work],
        compiler_params=limit(16),
        cost_estimate=pl.CostEstimate(flops=20_000_000, bytes_accessed=20_000_000, transcendentals=0),
        name="interior",
    )(vel, lm, mm, up, slab, points, xlow, xhigh, ulow, uhigh)
    shape = (CX, CY, NZ)
    shapes = [shape, shape, shape, (3, *shape)]
    _, _, eu, tv, ta = handed
    own = [tv, ta, eu, *sizes, CX * 16, 19 * 8]
    own = [pltpu.VMEM((n, 128), F32) for n in own] + [pltpu.SMEM((24,), jnp.int32)]
    cost = pl.CostEstimate(flops=4_000_000, bytes_accessed=4_000_000, transcendentals=0)
    *low, lm_next, mm_next, visc, body = pl.pallas_call(
        edge_low,
        out_shape=[rows(3 * 64)] * 2 + [pltpu.HBM(s, F32) for s in shapes],
        in_specs=[VMEM] * 10,
        out_specs=[VMEM] * 2 + [HBM] * 4,
        scratch_shapes=own + [pltpu.SemaphoreType.DMA((4,))],
        compiler_params=limit(16),
        cost_estimate=cost,
        name="edge_low",
    )(up, first[2], ylow, *first[3:8], *first[:2])
    given = [
        pltpu.with_memory_space_constraint(value, pltpu.HBM)
        for value in (lm_next, mm_next, visc, body)
    ]
    return pl.pallas_call(
        edge_high,
        out_shape=[pltpu.HBM(s, F32) for s in shapes],
        in_specs=[VMEM] * 10 + [HBM] * 4,
        out_specs=[HBM] * 4,
        input_output_aliases={10 + i: i for i in range(4)},
        scratch_shapes=own
        + [pltpu.VMEM((3 * 64, 128), F32)] * 2
        + [pltpu.SemaphoreType.DMA((8,))],
        compiler_params=limit(16),
        cost_estimate=cost,
        name="edge_high",
    )(up, first[2], yhigh, *first[8:13], *low, *given)


def solution(mesh):
    return jax.shard_map(
        shards,
        mesh=mesh,
        in_specs=(
            P(None, "gx", "gy", None),
            P("gx", "gy", None),
            P("gx", "gy", None),
            P(None, "gx", "gy", None),
            P("gx", "gy", None, None),
            P("gx", "gy", None),
            P("gx", "gy"),
        ),
        out_specs=(
            P("gx", "gy", None),
            P("gx", "gy", None),
            P("gx", "gy", None),
            P(None, "gx", "gy", None),
        ),
        check_vma=False,
    )
```

```python
import math

import jax
import jax.numpy as jnp
from jax import lax
from jax.experimental import pallas as pl
from jax.experimental.pallas import tpu as pltpu
from jax.sharding import PartitionSpec as P

F32 = jnp.float32
CX, CY, NZ = 8, 32, 128
TURBINES, SLOTS = 3, 192
ZLOW, ZSPAN = 46, 40
XMSG = 496
YMSG = 272
YA, YU, YN, YP = 72, 156, 210, 224
EY = 40
PY = 48


def shifted(block, axis, distance):
    count = lax.axis_size(axis)
    return lax.ppermute(block, axis, [(i, (i + distance) % count) for i in range(count)])


def weight(offset):
    scaled = offset * (1.0 / 1.5)
    return jnp.maximum(jnp.exp(-(scaled * scaled)) - math.exp(-4.0), 0.0)


def packed(parts):
    lane = lax.broadcasted_iota(jnp.int32, parts[0].shape, 1)
    first = pltpu.roll(parts[0], NZ - ZLOW, 1)
    second = pltpu.roll(parts[1], NZ + ZSPAN - ZLOW, 1)
    third = pltpu.roll(parts[2], 2 * ZSPAN - ZLOW, 1)
    rest = jnp.where(lane < 3 * ZSPAN, third, 0.0)
    return jnp.where(lane < ZSPAN, first, jnp.where(lane < 2 * ZSPAN, second, rest))


def pack_x(
    vel_in, lm_in, mm_in, pos_in, coef_in, count_in,
    low, high, slab, points, vel, lm, mm, pos, coef, count, sems,
):
    pairs = (
        (vel_in, vel), (pos_in, pos), (coef_in, coef), (count_in, count), (lm_in, lm), (mm_in, mm),
    )
    copies = [pltpu.make_async_copy(x, y, sems.at[i]) for i, (x, y) in enumerate(pairs)]
    for copy in copies:
        copy.start()
    for copy in copies[1:4]:
        copy.wait()
    lane = lax.broadcasted_iota(jnp.int32, (1, 128), 1)
    turbine_count = jnp.broadcast_to(count[...], (1, 128))
    early = lane < 64
    for t in range(TURBINES):
        at = t * SLOTS
        (pos_x, _), (y_first, y_rest), (z_first, z_rest), (s_first, s_rest) = [
            (values[:, at : at + 128], values[:, at + 64 : at + 192])
            for values in (pos[0], pos[1], pos[2], coef[...])
        ]
        live = turbine_count > t
        lines = [
            y_first,
            z_first,
            jnp.where(live, s_first, 0.0),
            jnp.where(early, pltpu.roll(z_rest, 64, 1), y_rest),
            jnp.where(early, pos_x, jnp.where(live, s_rest, 0.0)),
        ]
        block = jnp.concatenate(lines, axis=0)
        for out, base in ((low, 480), (high, 480), (points, 0)):
            out[pl.ds(base + 5 * t, 5), :] = block
    for out, base in ((low, 495), (high, 495), (points, 15)):
        out[pl.ds(base, 1), :] = jnp.zeros((1, 128), F32)
    copies[0].wait()
    for row in range(CX):
        parts = [vel[pl.ds((c * CX + row) * CY, CY), :] for c in range(3)]
        value = packed(parts)
        slab[pl.ds(row * CY, CY), :] = value
        if 2 <= row < 5:
            low[pl.ds(384 + (row - 2) * CY, CY), :] = value
        if 3 <= row < 6:
            high[pl.ds(384 + (row - 3) * CY, CY), :] = value
        for out, first in ((low, 0), (high, CX - 2)):
            if first <= row < first + 2:
                for c in range(3):
                    out[pl.ds(c * 64 + (row - first) * CY, CY), :] = parts[c]
    copies[4].wait()
    copies[5].wait()
    for out, first in ((low, 0), (high, CX - 3)):
        for f, own in enumerate((lm, mm)):
            out[pl.ds(192 + f * 96, 96), :] = own[pl.ds(first * CY, 96), :]


def pack_y(vel, lm, mm, slab, points, xlow, xhigh, low, high, ulow, uhigh):
    for out, message in ((ulow, xlow), (uhigh, xhigh)):
        for i in range(2):
            parts = [message[pl.ds(c * 64 + i * CY, CY), :] for c in range(3)]
            out[pl.ds(i * CY, CY), :] = packed(parts)
    for out, col_v, col_a, col_u in ((low, 0, 0, 0), (high, CY - 2, CY - 3, CY - 5)):
        for c in range(3):
            for j in range(2):
                base, col = (c * 2 + j) * 12, col_v + j
                out[pl.ds(base, 2), :] = xlow[pl.ds(c * 64 + col, 2, stride=CY), :]
                out[pl.ds(base + 2, 8), :] = vel[pl.ds(c * 256 + col, 8, stride=CY), :]
                out[pl.ds(base + 10, 2), :] = xhigh[pl.ds(c * 64 + col, 2, stride=CY), :]
        for f, own in enumerate((lm, mm)):
            for j in range(3):
                base, col = YA + (f * 3 + j) * 14, col_a + j
                out[pl.ds(base, 3), :] = xlow[pl.ds(192 + f * 96 + col, 3, stride=CY), :]
                out[pl.ds(base + 3, 8), :] = own[pl.ds(col, 8, stride=CY), :]
                out[pl.ds(base + 11, 3), :] = xhigh[pl.ds(192 + f * 96 + col, 3, stride=CY), :]
        far, near = (col_u, col_u + 3) if col_v else (col_u + 2, col_u)
        for j in range(3):
            base, col = YU + j * 18, far + j
            out[pl.ds(base, 3), :] = xlow[pl.ds(384 + col, 3, stride=CY), :]
            out[pl.ds(base + 3, 2), :] = ulow[pl.ds(col, 2, stride=CY), :]
            out[pl.ds(base + 5, 8), :] = slab[pl.ds(col, 8, stride=CY), :]
            out[pl.ds(base + 13, 2), :] = uhigh[pl.ds(col, 2, stride=CY), :]
            out[pl.ds(base + 15, 3), :] = xhigh[pl.ds(384 + col, 3, stride=CY), :]
        for j in range(2):
            base, col = YN + j * 6, near + j
            out[pl.ds(base, 3), :] = xlow[pl.ds(384 + col, 3, stride=CY), :]
            out[pl.ds(base + 3, 3), :] = xhigh[pl.ds(384 + col, 3, stride=CY), :]
        out[pl.ds(YN + 12, 2), :] = jnp.zeros((2, 128), F32)
        for k, source in enumerate((points, xlow, xhigh)):
            first = 0 if k == 0 else 480
            out[pl.ds(YP + 15 * k, 15), :] = source[pl.ds(first, 15), :]
        out[pl.ds(YP + 45, 3), :] = jnp.zeros((3, 128), F32)


def expand(source, base, out, out_base, count):
    early = lax.broadcasted_iota(jnp.int32, (1, 128), 1) < 64
    for t in range(count):
        block = source[pl.ds(base + 5 * t, 5), :]
        turned = pltpu.roll(block[3:5, :], 64, 1)
        lines = [
            block[0:1, :],
            block[3:4, :],
            block[1:2, :],
            turned[0:1, :],
            block[2:3, :],
            jnp.where(early, 0.0, block[4:5, :]),
            jnp.where(early, block[4:5, :], turned[1:2, :]),
            jnp.where(early, block[4:5, :], turned[1:2, :]),
        ]
        out[pl.ds(out_base + 8 * t, 8), :] = jnp.concatenate(lines, axis=0)


class Frame:
    def __init__(self, planes, width, turned):
        self.planes, self.width, self.turned = planes, width, turned

    def velocity(self, c, plane, cell):
        return (c * (self.planes + 4) + plane + 2) * self.width + cell + 4

    def average(self, f, plane, cell):
        return (f * (self.planes + 6) + plane + 3) * self.width + cell + 4

    def summed(self, q, plane, cell):
        return (q * (self.planes + 2) + plane + 1) * self.width + cell + 4

    def magnitude(self, plane, cell):
        return plane * self.width + cell + 4

    def sizes(self):
        n, w = self.planes, self.width
        return 3 * (n + 4) * w, 2 * (n + 6) * w, 15 * (n + 2) * w, 3 * (n + 2) * w, n * w


ROWS = Frame(CX, EY, False)
SIDE = Frame(3, 16, True)


def assemble(vel, lm, mm, slab, xlow, xhigh, ulow, uhigh, ev, ea, eu, ends):
    for c in range(3):
        for row in range(CX):
            ev[pl.ds(ROWS.velocity(c, row, 0), CY), :] = vel[pl.ds((c * CX + row) * CY, CY), :]
        for i in range(2):
            ev[pl.ds(ROWS.velocity(c, i - 2, 0), CY), :] = xlow[pl.ds(c * 64 + i * CY, CY), :]
            ev[pl.ds(ROWS.velocity(c, i + 8, 0), CY), :] = xhigh[pl.ds(c * 64 + i * CY, CY), :]
    for f, own in enumerate((lm, mm)):
        for row in range(CX):
            ea[pl.ds(ROWS.average(f, row, 0), CY), :] = own[pl.ds(row * CY, CY), :]
        for i in range(3):
            source = 192 + f * 96 + i * CY
            ea[pl.ds(ROWS.average(f, i - 3, 0), CY), :] = xlow[pl.ds(source, CY), :]
            ea[pl.ds(ROWS.average(f, i + 8, 0), CY), :] = xhigh[pl.ds(source, CY), :]
    zero = jnp.zeros((8, 128), F32)
    for row in range(18):
        eu[pl.ds(row * PY, 8), :] = zero
        eu[pl.ds(row * PY + 40, 8), :] = zero
    for row in range(CX):
        eu[pl.ds((row + 5) * PY + 8, CY), :] = slab[pl.ds(row * CY, CY), :]
    for i in range(3):
        eu[pl.ds(i * PY + 8, CY), :] = xlow[pl.ds(384 + i * CY, CY), :]
        eu[pl.ds((i + 15) * PY + 8, CY), :] = xhigh[pl.ds(384 + i * CY, CY), :]
    for i in range(2):
        eu[pl.ds((i + 3) * PY + 8, CY), :] = ulow[pl.ds(i * CY, CY), :]
        eu[pl.ds((i + 13) * PY + 8, CY), :] = uhigh[pl.ds(i * CY, CY), :]
    for end, (packed_end, tv, ta) in enumerate(ends):
        first = end * (CY - 3)
        for c in range(3):
            for plane in range(-2, 3) if end else range(5):
                source, target = ROWS.velocity(c, 0, first + plane), SIDE.velocity(c, plane, 0)
                for start, count in ((-2, 8), (6, 4)):
                    tv[pl.ds(target + start, count), :] = ev[
                        pl.ds(source + start * EY, count, stride=EY), :
                    ]
        for f in range(2):
            for plane in range(-3, 3) if end else range(6):
                source, target = ROWS.average(f, 0, first + plane), SIDE.average(f, plane, 0)
                for start, count in ((-3, 8), (3, 8)):
                    ta[pl.ds(target + start, count), :] = ea[
                        pl.ds(source + start * EY, count, stride=EY), :
                    ]
        for row in range(18):
            packed_end[pl.ds(row * 16, 16), :] = eu[pl.ds(row * PY + end * 32, 16), :]


def complete(end, message, eu, tv, ta):
    plane_v, plane_a, first = (3, 3, 8) if end else (-2, -3, 3)
    for c in range(3):
        for j in range(2):
            target = SIDE.velocity(c, plane_v + j, -2)
            tv[pl.ds(target, 12), :] = message[pl.ds((c * 2 + j) * 12, 12), :]
    for f in range(2):
        for j in range(3):
            target = SIDE.average(f, plane_a + j, -3)
            ta[pl.ds(target, 14), :] = message[pl.ds(YA + (f * 3 + j) * 14, 14), :]
    far, near = (first + 2, first) if end else (first, first + 3)
    for j in range(3):
        for start, count in ((0, 8), (8, 8), (16, 2)):
            eu[pl.ds(start * 16 + far + j, count, stride=16), :] = message[
                pl.ds(YU + j * 18 + start, count), :
            ]
    for j in range(2):
        for start, source in ((0, 0), (15, 3)):
            eu[pl.ds(start * 16 + near + j, 3, stride=16), :] = message[
                pl.ds(YN + j * 6 + source, 3), :
            ]
        for start, count in ((0, 8), (8, 4)):
            parts = [message[pl.ds((c * 2 + j) * 12 + start, count), :] for c in range(3)]
            eu[pl.ds((start + 3) * 16 + near + j, count, stride=16), :] = packed(parts)


PAIRS = ((0, 0), (1, 1), (2, 2), (0, 1), (0, 2), (1, 2))


def slope_z(values):
    lane = lax.broadcasted_iota(jnp.int32, values.shape, 1)
    above = jnp.where(lane == NZ - 1, values, pltpu.roll(values, NZ - 1, 1))
    below = jnp.where(lane == 0, values, pltpu.roll(values, 1, 1))
    return above - below


def tensor_of(slopes):
    parts = [slopes[0][0], slopes[1][1], slopes[2][2]]
    parts += [slopes[j][i] + slopes[i][j] for i, j in PAIRS[3:]]
    diag = parts[0] * parts[0] + parts[1] * parts[1] + parts[2] * parts[2]
    off = parts[3] * parts[3] + parts[4] * parts[4] + parts[5] * parts[5]
    return parts, jnp.sqrt(2.0 * diag + off)


def closure_first(frame, ev, xs, mags, starts):
    def at(c, plane, cell):
        return ev[pl.ds(frame.velocity(c, plane, cell), 8), :]

    def put(q, plane, cell, value):
        xs[pl.ds(frame.summed(q, plane, cell), 8), :] = value

    for cell in starts:
        before = [at(c, -2, cell) for c in range(3)]
        here = [at(c, -1, cell) for c in range(3)]
        history = []
        for plane in range(-1, frame.planes + 1):
            after = [at(c, plane + 1, cell) for c in range(3)]
            slopes = [
                [after[c] - before[c] for c in range(3)],
                [at(c, plane, cell + 1) - at(c, plane, cell - 1) for c in range(3)],
            ]
            if frame.turned:
                slopes.reverse()
            slopes.append([slope_z(here[c]) for c in range(3)])
            parts, mag = tensor_of(slopes)
            now = [mag * part for part in parts] + [here[i] * here[j] for i, j in PAIRS]
            if 0 <= plane < frame.planes:
                mags[pl.ds(frame.magnitude(plane, cell), 8), :] = mag
            for c in range(3):
                put(12 + c, plane, cell, before[c] + (here[c] + here[c]) + after[c])
            history.append(now)
            if len(history) == 3:
                for q in range(12):
                    value = history[0][q] + (history[1][q] + history[1][q]) + history[2][q]
                    put(q, plane - 1, cell, value)
                history.pop(0)
            before, here = here, after


def closure_hat(frame, xs, uh, starts):
    for c in range(3):
        for plane in range(-1, frame.planes + 1):
            for cell in starts:
                base = frame.summed(12 + c, plane, cell)
                mid = xs[pl.ds(base, 8), :]
                value = xs[pl.ds(base - 1, 8), :] + (mid + mid) + xs[pl.ds(base + 1, 8), :]
                uh[pl.ds(frame.summed(c, plane, cell), 8), :] = value


def take_rows(values, index):
    return jnp.take_along_axis(values, index, axis=0)


def averages_up(frame, ea, shift_plane, shift_cell, plane, cell):
    sub = lax.broadcasted_iota(jnp.int32, (8, 128), 0)
    index = sub - shift_cell + 3
    early = index < 8
    first = jnp.minimum(index, 7)
    second = jnp.maximum(index - 6, 0)
    result = [None, None]
    for shift in range(-3, 4):
        chosen = shift_plane == shift
        for f in range(2):
            base = frame.average(f, plane - shift, cell)
            value = jnp.where(
                early,
                take_rows(ea[pl.ds(base - 3, 8), :], first),
                take_rows(ea[pl.ds(base + 3, 8), :], second),
            )
            result[f] = value if result[f] is None else jnp.where(chosen, value, result[f])
    return result


def closure_last(frame, ea, up, xs, uh, mags, outs, starts, first=0, skipped=0):
    def summed(q, plane, cell):
        base = frame.summed(q, plane, cell)
        mid = xs[pl.ds(base, 8), :]
        return xs[pl.ds(base - 1, 8), :] + (mid + mid) + xs[pl.ds(base + 1, 8), :]

    def hat(c, plane, cell):
        return uh[pl.ds(frame.summed(c, plane, cell), 8), :]

    for plane in range(frame.planes):
        for cell in starts:
            here = [hat(c, plane, cell) for c in range(3)]
            slopes = [
                [hat(c, plane + 1, cell) - hat(c, plane - 1, cell) for c in range(3)],
                [hat(c, plane, cell + 1) - hat(c, plane, cell - 1) for c in range(3)],
            ]
            shifts = [
                pl.ds(d * CX * CY + plane * CY + cell, 8)
                if not frame.turned
                else pl.ds(d * CX * CY + cell * CY + first + plane, 8, stride=CY)
                for d in range(2)
            ]
            if frame.turned:
                slopes.reverse()
                shifts.reverse()
            slopes.append([slope_z(here[c]) for c in range(3)])
            parts, mag = tensor_of(slopes)
            mag = 0.25 * mag
            lm_sum = diag = off = None
            for q, (i, j) in enumerate(PAIRS):
                model = summed(q, plane, cell) - mag * parts[q]
                leonard = summed(6 + q, plane, cell) - (1.0 / 16.0) * (here[i] * here[j])
                term = leonard * model
                lm_sum = term if lm_sum is None else lm_sum + term
                square = model * model
                if q < 3:
                    diag = square if diag is None else diag + square
                else:
                    off = square if off is None else off + square
            lm_term = lm_sum * (1.0 / 512.0)
            mm_term = (2.0 * diag + off) * (1.0 / 2048.0)
            lm_up, mm_up = averages_up(frame, ea, up[shifts[0], :], up[shifts[1], :], plane, cell)
            ratio = (0.2 / 1.5) * jnp.sqrt(jnp.sqrt(jnp.sqrt(lm_up * mm_up)))
            inverse = 1.0 / (1.0 + ratio)
            lm_new = jnp.maximum((ratio * lm_term + lm_up) * inverse, 0.0)
            mm_new = (ratio * mm_term + mm_up) * inverse
            smag = 0.5 * mags[pl.ds(frame.magnitude(plane, cell), 8), :]
            if frame.turned:
                where_at = pl.ds(skipped + plane, 8, stride=8)
            else:
                where_at = pl.ds(plane * CY + cell, 8)
            for out, value in zip(outs, (lm_new, mm_new, lm_new / mm_new * smag)):
                out[where_at, :] = value


def split(values):
    high = values.astype(jnp.bfloat16)
    return high, (values - high.astype(F32)).astype(jnp.bfloat16)


def dot_over(a, b, dims):
    (a_high, a_low), (b_high, b_low) = split(a), split(b)

    def dot(x, y):
        return lax.dot_general(x, y, (dims, ((), ())), preferred_element_type=F32)

    return dot(a_high, b_high) + dot(a_high, b_low) + dot(a_low, b_high)


def turbines(blocks, shift_x, shift_y, in_rows, first, span, out_rows, out_at, eu, total, keep):
    begin, stride, columns_out = out_at
    cell_x = lax.broadcasted_iota(jnp.int32, (24, 128), 0).astype(F32) - 5.0 - shift_x
    cell_y = lax.broadcasted_iota(jnp.int32, (span, 256), 0).astype(F32) + shift_y
    cell_z = lax.broadcasted_iota(jnp.int32, (ZSPAN, 256), 0).astype(F32) + float(ZLOW)
    weights_x = [weight(cell_x - block[6:7, :]) for block in blocks]
    planes = [None] * len(blocks)
    for row in in_rows:
        values = eu[pl.ds((row + 5) * PY + first, span), :]
        for t, weight_x in enumerate(weights_x):
            term = weight_x[row + 5 : row + 6, :] * values
            planes[t] = term if planes[t] is None else planes[t] + term
    patches = []
    for block, plane in zip(blocks, planes):
        pos_y = jnp.concatenate([block[0:1, :], block[1:2, :]], axis=1)
        pos_z = jnp.concatenate([block[2:3, :], block[3:4, :]], axis=1)
        strength = jnp.concatenate([block[4:5, :], block[5:6, :]], axis=1)
        strength = jnp.where(keep(pos_y), strength, 0.0)
        weight_y = weight(cell_y - pos_y)
        weight_z = weight(cell_z - pos_z)
        columns = dot_over(plane.T, weight_y, ((1,), (0,)))
        sampled = [
            jnp.sum(columns[c * ZSPAN : (c + 1) * ZSPAN, :] * weight_z, axis=0, keepdims=True)
            for c in range(3)
        ]
        speed = jnp.sqrt(sampled[0] * sampled[0] + sampled[1] * sampled[1] + sampled[2] * sampled[2])
        scale = -(strength * speed)
        spread = [weight_z * (scale * sampled[c]) for c in range(3)]
        spread = jnp.concatenate(spread + [jnp.zeros((8, 256), F32)], axis=0)
        rows_y = weight_y[8 : 8 + CY, :] if columns_out == CY else weight_y
        patches.append(dot_over(rows_y, spread, ((1,), (1,))))
    for row in out_rows:
        where_at = pl.ds(row * stride + begin, columns_out)
        value = total[where_at, :]
        for weight_x, patch in zip(weights_x, patches):
            value = value + weight_x[row + 5 : row + 6, :] * patch
        total[where_at, :] = value


def inside(pos_y):
    return (pos_y >= 2.0) & (pos_y <= float(CY - 3))


def unpack(values):
    lane = lax.broadcasted_iota(jnp.int32, values.shape, 1)
    held = (lane >= ZLOW) & (lane < ZLOW + ZSPAN)
    shifts = (ZLOW, NZ + ZLOW - ZSPAN, NZ + ZLOW - 2 * ZSPAN)
    return [jnp.where(held, pltpu.roll(values, shift % NZ, 1), 0.0) for shift in shifts]


def interior(
    vel, lm, mm, up, slab, points, xlow, xhigh, ulow, uhigh,
    results, forces, expanded, *refs,
):
    ends = refs[:5], refs[5:10]
    ev, ea, xs, uh, mags, total, eu = refs[10:]
    assemble(vel, lm, mm, slab, xlow, xhigh, ulow, uhigh, ev, ea, eu, [end[2:] for end in ends])
    closure_first(ROWS, ev, xs, mags, (1, 9, 17, 23))
    closure_hat(ROWS, xs, uh, (2, 10, 18, 22))
    field = CX * CY
    outs = [results.at[pl.ds(i * field, field), :] for i in range(3)]
    closure_last(ROWS, ea, up, xs, uh, mags, outs, (3, 11, 19, 21))
    total[...] = jnp.zeros((field, 128), F32)
    for k, source in enumerate((points, xlow, xhigh)):
        expand(source, 480 if k else 0, expanded, 24 * k, TURBINES)
    for base, shift_x, in_rows, out_rows in (
        (0, 0.0, range(-2, 11), range(0, 8)),
        (24, -8.0, range(-5, 3), range(0, 3)),
        (48, 8.0, range(6, 13), range(6, 8)),
    ):
        blocks = [expanded[pl.ds(base + t * 8, 8), :] for t in range(TURBINES)]
        turbines(blocks, shift_x, -8.0, in_rows, 0, PY, out_rows, (0, CY, CY), eu, total, inside)
    for row in range(CX):
        values = total[pl.ds(row * CY, CY), :]
        for c, out in enumerate(unpack(values)):
            forces[pl.ds((c * CX + row) * CY, CY), :] = out
        for end, (rim, total_rim, *_) in enumerate(ends):
            col = end * (CY - 8)
            total_rim[pl.ds(row * 16 + 8 - 8 * end, 8), :] = values[col : col + 8, :]
            for i in range(3):
                rim[pl.ds((i * CX + row) * 8, 8), :] = results[
                    pl.ds(i * field + row * CY + col, 8), :
                ]


def rim_hits(end, everyone):
    lines = []
    place = lax.broadcasted_iota(jnp.int32, (9, 128), 0)
    left = (place >= 3) & (place < 6)
    least, most = jnp.where(left, 5.0, -1.0), jnp.where(place < 6, float(CX + 1), 2.0)
    for beyond in range(2):

        def line(q, base=72 * beyond):
            parts = everyone[pl.ds(base + q, 8, stride=8), :], everyone[pl.ds(base + 64 + q, 1), :]
            return jnp.concatenate(parts, axis=0)

        hit = None
        for half in range(2):
            pos_y = line(half)
            found = (pos_y > float(CY - 3)) if end != beyond else (pos_y < 2.0)
            found = found & (line(4 + half) > 0.0)
            hit = found if hit is None else hit | found
        pos_x = line(6)
        hit = hit & (pos_x > least) & (pos_x < most)
        lines.append(jnp.max(hit.astype(F32), axis=1, keepdims=True))
    bits = lax.shift_left(
        jnp.ones((9, 1), jnp.int32), lax.broadcasted_iota(jnp.int32, (9, 1), 0)
    ).astype(F32)
    return jnp.sum(bits * (lines[0] + 512.0 * lines[1])).astype(jnp.int32)


def stacked_product(a, b, dims, axes):
    (a_high, a_low), (b_high, b_low) = split(a), split(b)
    a_terms = jnp.concatenate([a_high, a_high, a_low], axis=axes[0])
    b_terms = jnp.concatenate([b_high, b_low, b_high], axis=axes[1])
    return lax.dot_general(a_terms, b_terms, (dims, ((), ())), preferred_element_type=F32)


def rim_batch(end, items, eu, total, everyone):
    cell_x = lax.broadcasted_iota(jnp.int32, (24, 128), 0).astype(F32) - 5.0
    cell_y = lax.broadcasted_iota(jnp.int32, (16, 256), 0).astype(F32)
    cell_z = lax.broadcasted_iota(jnp.int32, (ZSPAN, 256), 0).astype(F32) + float(ZLOW)
    ready = []
    for item in items:
        beyond = item >= 9
        place = jnp.where(beyond, item - 9, item)
        block = everyone[pl.ds(pl.multiple_of(item * 8, 8), 8), :]
        shift_x = jnp.where(place < 3, 0.0, jnp.where(place < 6, -8.0, 8.0))
        late = jnp.logical_not(beyond) if end else beyond
        shift_y = jnp.where(late, 24.0, -8.0)
        lowest = jnp.where(late, float(CY - 3), -1.0)
        highest = jnp.where(late, float(CY + 1), 2.0)
        weight_x = weight(cell_x - shift_x - block[6:7, :])
        terms = [weight_x[row : row + 1, :] * eu[pl.ds(row * 16, 16), :] for row in range(18)]
        while len(terms) > 1:
            terms = [sum(terms[i + 1 : i + 2], terms[i]) for i in range(0, len(terms), 2)]
        pos_y = jnp.concatenate([block[0:1, :], block[1:2, :]], axis=1)
        pos_z = jnp.concatenate([block[2:3, :], block[3:4, :]], axis=1)
        strength = jnp.concatenate([block[4:5, :], block[5:6, :]], axis=1)
        strength = jnp.where((pos_y > lowest) & (pos_y < highest), strength, 0.0)
        weights = weight(cell_y + shift_y - pos_y), weight(cell_z - pos_z)
        ready.append((weight_x, terms[0], *weights, strength))
    patches = []
    for _, plane, weight_y, weight_z, strength in ready:
        columns = stacked_product(plane.T, weight_y, ((1,), (0,)), (1, 0))
        sampled = [
            jnp.sum(columns[c * ZSPAN : (c + 1) * ZSPAN, :] * weight_z, axis=0, keepdims=True)
            for c in range(3)
        ]
        speed = jnp.sqrt(sampled[0] * sampled[0] + sampled[1] * sampled[1] + sampled[2] * sampled[2])
        scale = -(strength * speed)
        spread = [weight_z * (scale * sampled[c]) for c in range(3)]
        spread = jnp.concatenate(spread + [jnp.zeros((8, 256), F32)], axis=0)
        patches.append(stacked_product(weight_y, spread, ((1,), (1,)), (1, 1)))
    for row in range(CX):
        value = total[pl.ds(row * 16, 16), :]
        for patch, (weight_x, *_) in zip(patches, ready):
            value = value + weight_x[row + 5 : row + 6, :] * patch
        total[pl.ds(row * 16, 16), :] = value


def finish(end, inputs, scratch, results, forces, closed):
    up, expanded, message, rim_in, total_in, eu_in, tv_in, ta_in = inputs
    tv, ta, eu, xs, uh, mags, total, everyone, listed = scratch
    everyone[pl.ds(0, 72), :] = expanded[...]
    expand(message, YP, everyone, 72, 3 * TURBINES)
    everyone[pl.ds(144, 8), :] = jnp.zeros((8, 128), F32)
    hits = rim_hits(end, everyone)
    found = jnp.int32(0)
    for item in range(18):
        listed[found] = jnp.int32(item)
        found = found + lax.rem(lax.shift_right_logical(hits, item), 2)
    for i in range(3):
        listed[found + i] = jnp.int32(18)
    tv[...] = tv_in[...]
    ta[...] = ta_in[...]
    eu[...] = eu_in[...]
    total[...] = total_in[...]
    results[...] = rim_in[...]
    complete(end, message, eu, tv, ta)
    closure_first(SIDE, tv, xs, mags, (-2, 2))
    closure_hat(SIDE, xs, uh, (-1, 1))
    outs = [results.at[pl.ds(i * 64, 64), :] for i in range(3)]
    first, skipped = (CY - 3, 5) if end else (0, 0)
    closure_last(SIDE, ta, up, xs, uh, mags, outs, (0,), first, skipped)
    closed()

    def batch(i, carry):
        rim_batch(end, [listed[3 * i + t] for t in range(3)], eu, total, everyone)
        return carry

    @pl.when(found == 1)
    def _():
        rim_batch(end, [listed[0]], eu, total, everyone)

    @pl.when(found > 1)
    def _():
        lax.fori_loop(0, lax.div(found + 2, 3), batch, 0)

    for row in range(CX):
        values = total[pl.ds(row * 16 + 8 - 8 * end, 8), :]
        for c, out in enumerate(unpack(values)):
            forces[pl.ds((c * CX + row) * 8, 8), :] = out


def edge_low(*refs):
    finish(0, refs[:8], refs[10:], refs[8], refs[9], lambda: None)


def edge_high(*refs):
    low_results, low_forces, inner_results, inner_forces = refs[8:12]
    targets, scratch = refs[12:16], refs[16:25]
    results, forces, sems = refs[25:]
    copies = []

    def send(source, target, first, count):
        target = target.at[..., pl.ds(first, count), :]
        copies.append(pltpu.make_async_copy(source, target, sems.at[len(copies)]))
        copies[-1].start()

    def fields(values, first):
        for i, target in enumerate(targets[:3]):
            send(values.at[pl.ds(i * 64, 64), :].reshape(CX, 8, NZ), target, first, 8)

    middle = pl.ds(8, CY - 16)
    send(inner_forces.reshape(3, CX, CY, NZ).at[:, :, middle, :], targets[3], 8, CY - 16)
    part = CX * CY
    for i, target in enumerate(targets[:3]):
        source = inner_results.at[pl.ds(i * part, part), :].reshape(CX, CY, NZ)
        send(source.at[:, middle, :], target, 8, CY - 16)
    fields(low_results, 0)
    send(low_forces.reshape(3, CX, 8, NZ), targets[3], 0, 8)
    finish(1, refs[:8], scratch, results, forces, lambda: fields(results, CY - 8))
    send(forces.reshape(3, CX, 8, NZ), targets[3], CY - 8, 8)
    for copy in copies:
        copy.wait()


VMEM = pl.BlockSpec(memory_space=pltpu.VMEM)
HBM = pl.BlockSpec(memory_space=pltpu.HBM)


def rows(count):
    return jax.ShapeDtypeStruct((count, 128), F32)


def limit(mebibytes):
    return pltpu.CompilerParams(vmem_limit_bytes=mebibytes * 1024 * 1024)


def shards(velocity, lm_old, mm_old, upstream, point_pos, point_coef, tile_turbines):
    field = CX * CY
    up = upstream.reshape(2 * field, NZ)
    inputs = (
        velocity.reshape(3 * field, NZ),
        lm_old.reshape(field, NZ),
        mm_old.reshape(field, NZ),
        point_pos.reshape(3, 1, TURBINES * SLOTS),
        point_coef[0],
    )
    low, high, slab, points, vel, lm, mm = pl.pallas_call(
        pack_x,
        out_shape=[rows(n) for n in (XMSG, XMSG, field, 16, 3 * field, field, field)],
        in_specs=[HBM] * 5 + [pl.BlockSpec(memory_space=pl.ANY)],
        out_specs=[VMEM] * 7,
        scratch_shapes=[
            pltpu.VMEM((3, 1, TURBINES * SLOTS), F32),
            pltpu.VMEM((1, TURBINES * SLOTS), F32),
            pltpu.VMEM((1, 1), jnp.int32),
            pltpu.SemaphoreType.DMA((6,)),
        ],
        compiler_params=limit(8),
        name="pack_x",
    )(*(pltpu.with_memory_space_constraint(value, pltpu.HBM) for value in inputs), tile_turbines)
    xlow = shifted(high, "gx", 1)
    xhigh = shifted(low, "gx", -1)
    low, high, ulow, uhigh = pl.pallas_call(
        pack_y,
        out_shape=(rows(YMSG), rows(YMSG), rows(64), rows(64)),
        in_specs=[VMEM] * 7,
        out_specs=(VMEM,) * 4,
        compiler_params=limit(8),
        name="pack_y",
    )(vel, lm, mm, slab, points, xlow, xhigh)
    ylow = shifted(high, "gy", 1)
    yhigh = shifted(low, "gy", -1)
    size_v, size_a, *sizes = SIDE.sizes()
    handed = [3 * 64, CX * 16, 18 * 16, size_v, size_a]
    work = [*ROWS.sizes(), field, 18 * PY]
    first = pl.pallas_call(
        interior,
        out_shape=[rows(n) for n in (3 * field, 3 * field, 9 * 8, *handed, *handed)],
        in_specs=[VMEM] * 10,
        out_specs=[VMEM] * 13,
        scratch_shapes=[pltpu.VMEM((n, 128), F32) for n in work],
        compiler_params=limit(16),
        cost_estimate=pl.CostEstimate(flops=20_000_000, bytes_accessed=20_000_000, transcendentals=0),
        name="interior",
    )(vel, lm, mm, up, slab, points, xlow, xhigh, ulow, uhigh)
    shape = (CX, CY, NZ)
    shapes = [shape, shape, shape, (3, *shape)]
    _, _, eu, tv, ta = handed
    own = [tv, ta, eu, *sizes, CX * 16, 19 * 8]
    own = [pltpu.VMEM((n, 128), F32) for n in own] + [pltpu.SMEM((24,), jnp.int32)]
    cost = pl.CostEstimate(flops=4_000_000, bytes_accessed=4_000_000, transcendentals=0)
    low = pl.pallas_call(
        edge_low,
        out_shape=[rows(3 * 64)] * 2,
        in_specs=[VMEM] * 8,
        out_specs=[VMEM] * 2,
        scratch_shapes=own,
        compiler_params=limit(16),
        cost_estimate=cost,
        name="edge_low",
    )(up, first[2], ylow, *first[3:8])
    return pl.pallas_call(
        edge_high,
        out_shape=[pltpu.HBM(s, F32) for s in shapes],
        in_specs=[VMEM] * 12,
        out_specs=[HBM] * 4,
        scratch_shapes=own
        + [pltpu.VMEM((3 * 64, 128), F32)] * 2
        + [pltpu.SemaphoreType.DMA((12,))],
        compiler_params=limit(16),
        cost_estimate=cost,
        name="edge_high",
    )(up, first[2], yhigh, *first[8:13], *low, *first[:2])


def solution(mesh):
    return jax.shard_map(
        shards,
        mesh=mesh,
        in_specs=(
            P(None, "gx", "gy", None),
            P("gx", "gy", None),
            P("gx", "gy", None),
            P(None, "gx", "gy", None),
            P("gx", "gy", None, None),
            P("gx", "gy", None),
            P("gx", "gy"),
        ),
        out_specs=(
            P("gx", "gy", None),
            P("gx", "gy", None),
            P("gx", "gy", None),
            P(None, "gx", "gy", None),
        ),
        check_vma=False,
    )
```
